32 devices in a mesh: dp: 16 (over z, y, core), section: 2 (over x).
Axes of the slice: x: 2, y: 2, z: 4, core: 2. Of those that a mesh axis runs over, the one named last changes fastest.
Arguments:
- stream_in: bfloat16 [32768, 767], P(('dp', 'section')), may hold values from -60 to 60
- seq_len: int32 [16], P('dp'), may hold values from 256 to 1024, as said below
- live_rows: int32 [16], P('dp'), may hold values from 512 to 2048, as said below
- norm_gain: float32 [2, 768], P('section'), may hold values from 0.25 to 1.75
- first_weight: bfloat16 [2, 768, 3072], P('section'), may hold values from -5 to 5
- down_weight: bfloat16 [3072, 768], P('section'), may hold values from -0.109375 to 0.109375
- out_grad: bfloat16 [32768, 767], P(('dp', 'section')), may hold values from -6 to 6
Outputs:
- stream_out: bfloat16 [32768, 767], P(('dp', 'section'))
- stream_grad: bfloat16 [32768, 767], P(('dp', 'section'))
- gain_grad: float32 [2, 768], P('section', 'dp')
- first_grad: float32 [2, 768, 3072], P('section', None, 'dp')
- down_grad: float32 [3072, 768], P('section', 'dp')
The draws below stay inside these ranges and needn't reach their ends.
Inputs may be any that keep to these rules, and one draw needn't show every extreme that they name: `seq_len`: each bucket's sequence length is 256, 512 or 1024. `live_rows`: the live rows of a bucket are its first ones.
All inputs are finite; a program needn't handle non-finite values.
Results may differ from the reference program's by a relative error of at most 0.017.
Values may be sent and summed in bfloat16 or wider, within the bound.
A program may use at most 256 MiB of HBM per device.

```python
import jax
import jax.numpy as jnp
from jax import lax

D = 768
HEADS = 12
HEAD_DIM = 64
FF = 3072
MB_ROWS = 1024
STREAM = 767
BLOCK = 512
TOKENS = 32768
N_DP = 16


def draw_stream_in(key, part):
    base_key, row_key, col_key = jax.random.split(key, 3)
    shape = (TOKENS, D - 1)
    row_scale = jnp.exp(jax.random.uniform(row_key, (TOKENS, 1), jnp.float32, -1.15, 1.15))
    col_scale = jnp.exp(jax.random.uniform(col_key, (1, D - 1), jnp.float32, -1.15, 1.15))
    base = jax.random.normal(base_key, shape, jnp.float32)
    base = jnp.clip(base, -6.0, 6.0)
    return (base * row_scale * col_scale).astype(jnp.bfloat16)


def draw_first_weight(key, part):
    shape = (2, D, FF)
    base = jnp.clip(jax.random.normal(key, shape, jnp.float32), -6.0, 6.0)
    column = jnp.arange(FF, dtype=jnp.int32)
    which = jnp.arange(2, dtype=jnp.int32)
    boost = jnp.where((which[:, None, None] == 0) & (column[None, None, :] >= 3 * D), 8.0, 1.0)
    return (base * boost * D ** (-0.5)).astype(jnp.bfloat16)


def draw_seq_len(key, part):
    level_key, order_key = jax.random.split(jax.random.fold_in(key, 11))
    level = jax.random.randint(level_key, (N_DP,), 0, 3)
    lengths = jnp.where(level == 0, MB_ROWS // 4, jnp.where(level == 1, MB_ROWS // 2, MB_ROWS))
    order = jax.random.permutation(order_key, N_DP)
    lengths = lengths.at[order[0]].set(MB_ROWS).at[order[1]].set(MB_ROWS // 4)
    return lengths.astype(jnp.int32)


def draw_live_rows(key, part):
    count_key, order_key = jax.random.split(jax.random.fold_in(key, 23))
    counts = jax.random.randint(count_key, (N_DP,), MB_ROWS // 2, 2 * MB_ROWS + 1)
    order = jax.random.permutation(order_key, N_DP)
    counts = counts.at[order[0]].set(2 * MB_ROWS).at[order[1]].set(MB_ROWS // 2)
    return counts.astype(jnp.int32)


def level_of(own_key, dims, cuts, low, top_value):
    level = 1.0
    for dim, shards_of in cuts:
        steps = jax.random.uniform(jax.random.fold_in(jax.random.fold_in(own_key, 6), dim), (shards_of,), jnp.float32, low / len(cuts), top_value / len(cuts))
        level = level * jnp.repeat(jnp.exp(steps), dims[dim] // shards_of).reshape((-1,) + (1,) * (len(dims) - 1 - dim))
    return level


def scatter_about(stream_key, extent, scale, bound, cuts=(), kind=jnp.bfloat16):
    level = level_of(stream_key, extent, cuts, -0.22, 0.18) if cuts else 1.0
    entries = jax.random.normal(stream_key, extent, jnp.float32) * scale * level
    return jnp.minimum(jnp.maximum(entries, -bound), bound).astype(kind)


def setup_inputs(seed: int = 0) -> dict:
    keys = jax.random.split(jax.random.key(seed), 8)
    stream_in = draw_stream_in(jax.random.fold_in(keys[7], 71), 0)
    seq_len = draw_seq_len(jax.random.fold_in(keys[7], 71), 0)
    live_rows = draw_live_rows(jax.random.fold_in(keys[7], 71), 0)
    norm_gain = jnp.clip(1.0 + 0.15 * jax.random.normal(keys[3], (2, D), jnp.float32), 0.25, 1.75)
    first_weight = draw_first_weight(jax.random.fold_in(keys[7], 71), 0)
    down_weight = scatter_about(keys[5], (FF, D), FF ** -0.5, 0.109375, ((0, 2),))
    out_grad = scatter_about(keys[6], (TOKENS, STREAM), 1.0, 6.0, ((0, 32),))
    return {"stream_in": stream_in, "seq_len": seq_len, "live_rows": live_rows, "norm_gain": norm_gain, "first_weight": first_weight, "down_weight": down_weight, "out_grad": out_grad}


EPSILON = 1e-05
MASKED_SCORE = -1e+30

@jax.custom_vjp
def low(v):
    return lax.optimization_barrier(v.astype(jnp.bfloat16)).astype(jnp.float32)

@jax.custom_vjp
def low_back(v):
    return v

def low_keep(v):
    return (low(v), None)

def low_pass(kept, grad):
    return (grad,)

def back_keep(v):
    return (v, None)

def back_low(kept, grad):
    return (low(grad),)
low.defvjp(low_keep, low_pass)
low_back.defvjp(back_keep, back_low)

def product(left, right):
    return jnp.dot(left, right, precision=lax.Precision.HIGHEST, preferred_element_type=jnp.float32)

def center_norm(compact, gain):
    last = -lax.optimization_barrier(jnp.sum(compact, axis=-1, keepdims=True))
    full = jnp.concatenate([compact, last], axis=-1)
    scale = lax.rsqrt(lax.optimization_barrier(jnp.mean(full * full, axis=-1, keepdims=True)) + EPSILON)
    return full * scale * gain

def squeeze_branch(branch):
    return branch[:, :-1] - lax.optimization_barrier(jnp.mean(branch, axis=-1, keepdims=True))

def gelu_tanh(value):
    return jax.nn.gelu(value, approximate=True)

def attend(qkv, length, live_count):
    row_count = qkv.shape[0]
    width = qkv.shape[1] // 3
    query_all = qkv[:, :width].reshape(row_count, HEADS, HEAD_DIM)
    key_all = qkv[:, width:2 * width].reshape(row_count, HEADS, HEAD_DIM)
    value_all = qkv[:, 2 * width:].reshape(row_count, HEADS, HEAD_DIM)
    key_pos = jnp.arange(row_count, dtype=jnp.int32)
    scale = HEAD_DIM ** (-0.5)

    def one_block(first_row):
        query_block = lax.dynamic_slice_in_dim(query_all, first_row, BLOCK, 0)
        query_pos = first_row + jnp.arange(BLOCK, dtype=jnp.int32)
        raw = jnp.einsum('qhd,khd->hqk', query_block, key_all, precision=lax.Precision.HIGHEST)
        scores = low_back(raw) * scale
        same_doc = (query_pos // length)[:, None] == (key_pos // length)[None, :]
        causal = key_pos[None, :] <= query_pos[:, None]
        usable = (key_pos[None, :] < live_count) | (key_pos[None, :] == query_pos[:, None])
        allowed = same_doc & causal & usable
        scores = jnp.where(allowed[None], scores, MASKED_SCORE)
        top = lax.optimization_barrier(jnp.max(scores, axis=-1, keepdims=True))
        terms = jnp.exp(scores - top)
        probs = low(terms / lax.optimization_barrier(jnp.sum(terms, axis=-1, keepdims=True)))
        mixed = jnp.einsum('hqk,khd->qhd', probs, value_all, precision=lax.Precision.HIGHEST)
        return mixed.reshape(BLOCK, width)
    starts = jnp.arange(row_count // BLOCK, dtype=jnp.int32) * BLOCK
    return lax.map(jax.checkpoint(one_block), starts).reshape(row_count, width)

def block_forward(stream, gains, firsts, down, length, live_count):
    width = gains.shape[1]
    attn_weight = firsts[0]
    up_weight = firsts[1]
    norm_one = low(center_norm(stream, gains[0]))
    qkv = low_back(low(product(norm_one, attn_weight[:, :3 * width])))
    attn = low_back(low(attend(qkv, length, live_count)))
    branch_one = low_back(product(attn, attn_weight[:, 3 * width:]))
    stream_mid = low_back(low(stream + squeeze_branch(branch_one)))
    norm_two = low(center_norm(stream_mid, gains[1]))
    pre = low_back(product(norm_two, up_weight))
    act = low(gelu_tanh(pre))
    branch_two = low_back(product(act, down))
    live = (jnp.arange(stream.shape[0], dtype=jnp.int32) < live_count).astype(jnp.float32)[:, None]
    return (stream_mid + squeeze_branch(branch_two)) * live

def reference(stream_in, seq_len, live_rows, norm_gain, first_weight, down_weight, out_grad):
    count = 2 * N_DP
    streams = stream_in.astype(jnp.float32).reshape(count, MB_ROWS, STREAM)
    cotangents = out_grad.astype(jnp.float32).reshape(count, MB_ROWS, STREAM)
    gains = norm_gain.astype(jnp.float32)
    firsts = first_weight.astype(jnp.float32)
    down = down_weight.astype(jnp.float32)

    def step(totals, item):
        stream, cotangent, micro_index = item
        bucket = micro_index // 2
        micro_part = micro_index % 2
        length = seq_len[bucket]
        live_count = live_rows[bucket] - micro_part * MB_ROWS

        def layer(stream_value, gain_value, first_value, down_value):
            return block_forward(stream_value, gain_value, first_value, down_value, length, live_count)
        output, pullback = jax.vjp(layer, stream, gains, firsts, down)
        stream_back, gain_back, first_back, down_back = pullback(cotangent)
        totals = (totals[0] + gain_back, totals[1] + first_back, totals[2] + down_back)
        return (totals, (output, stream_back))
    start = (jnp.zeros(gains.shape, jnp.float32), jnp.zeros(firsts.shape, jnp.float32), jnp.zeros(down.shape, jnp.float32))
    totals, results = lax.scan(step, start, (streams, cotangents, jnp.arange(count, dtype=jnp.int32)))
    outputs, stream_backs = results
    stream_out = outputs.reshape(TOKENS, STREAM).astype(jnp.bfloat16)
    stream_grad = stream_backs.reshape(TOKENS, STREAM).astype(jnp.bfloat16)
    return (stream_out, stream_grad, totals[0], totals[1], totals[2])
```

```python
import functools

import jax
import jax.numpy as jnp
from jax import lax
from jax.experimental import pallas as pl
from jax.experimental.pallas import tpu as pltpu
from jax.sharding import PartitionSpec as P

HEADS = 12
HEAD_DIM = 64
EPSILON = 1e-05
MASKED_SCORE = -1e30
LANE = 128
TILE = 256
F32 = jnp.float32
BF16 = jnp.bfloat16
VMEM_LIMIT = 66000000


def dot(left, right):
    return lax.dot_general(left, right, (((1,), (0,)), ((), ())), preferred_element_type=F32)


def dot_rows(left, right):
    return lax.dot_general(left, right, (((1,), (1,)), ((), ())), preferred_element_type=F32)


def lane_of(shape):
    return lax.broadcasted_iota(jnp.int32, shape, 1)


def full_width(block):
    lane = lane_of(block.shape)
    last = block.shape[1] - 1
    kept = jnp.where(lane == last, 0.0, block)
    return jnp.where(lane == last, -jnp.sum(kept, axis=-1, keepdims=True), kept)


def norm_parts(block):
    full = full_width(block)
    scale = lax.rsqrt(jnp.mean(full * full, axis=-1, keepdims=True) + EPSILON)
    return full * scale, scale


def norm_back(fhat, scale, gain, grad):
    weighted = grad * gain
    inner = jnp.mean(weighted * fhat, axis=-1, keepdims=True)
    error = scale * (weighted - fhat * inner)
    last = error.shape[1] - 1
    tail = jnp.sum(jnp.where(lane_of(error.shape) == last, error, 0.0), axis=-1, keepdims=True)
    return error - tail


def drop_last(block):
    return jnp.where(lane_of(block.shape) == block.shape[1] - 1, 0.0, block)


def widen(block):
    return block - jnp.sum(block, axis=-1, keepdims=True) * (1.0 / block.shape[1])


def allowed_of(query_pos, key_pos, length, live_count):
    start = query_pos & (-length)
    usable = (key_pos < live_count) | (key_pos == query_pos)
    return (key_pos >= start) & (key_pos <= query_pos) & usable


def attention_kernel(
    info_ref, x_ref, gain_ref, w_ref, wo_ref, qkv_ref, attn_ref, lse_ref, mid_ref,
    norm_ref, bias_ref, cols_ref,
):
    rows, width = x_ref.shape
    steps = w_ref.shape[0]
    tiles = rows // TILE
    length, live_count = info_ref[0], info_ref[1]
    gain = gain_ref[...]

    def norm_step(tile, carry):
        at = pl.ds(tile * TILE, TILE)
        fhat, _ = norm_parts(x_ref[at, :].astype(F32))
        norm_ref[at, :] = (fhat * gain).astype(BF16)
        query = tile * TILE + lax.broadcasted_iota(jnp.int32, (TILE, rows), 0)
        key = lax.broadcasted_iota(jnp.int32, (TILE, rows), 1)
        bias_ref[at, :] = jnp.where(allowed_of(query, key, length, live_count), 0.0, MASKED_SCORE)
        return carry

    lax.fori_loop(0, tiles, norm_step, 0)
    cols_ref[...] = jnp.zeros_like(cols_ref)

    def step(p, carry):
        def project(tile, inner):
            at = pl.ds(tile * TILE, TILE)
            out = dot(norm_ref[at, :], w_ref[p]).astype(BF16)
            for t in range(3):
                for y in range(2):
                    lo = (2 * t + y) * LANE
                    qkv_ref[2 * p + y, t, at, :] = out[:, lo : lo + LANE]
            return inner

        lax.fori_loop(0, tiles, project, 0)

        def pair(y, inner):
            block = 2 * p + y
            first_head = 6 * y + 2 * p
            for qb in range(tiles):
                count = (qb + 1) * TILE
                at = pl.ds(qb * TILE, TILE)
                lane = lane_of((TILE, LANE))
                query = qkv_ref[block, 0, at, :] * BF16(HEAD_DIM**-0.5)
                keys = qkv_ref[block, 1, pl.ds(0, count), :]
                values = qkv_ref[block, 2, pl.ds(0, count), :]
                key_lane = lane_of((count, LANE))
                mixed = []
                for i in range(2):
                    mine = (lane < HEAD_DIM) if i == 0 else (lane >= HEAD_DIM)
                    key_mine = (key_lane < HEAD_DIM) if i == 0 else (key_lane >= HEAD_DIM)
                    scores = dot_rows(jnp.where(mine, query, BF16(0)), keys)
                    scores = scores + bias_ref[at, pl.ds(0, count)]
                    top = jnp.max(scores, axis=-1, keepdims=True)
                    terms = jnp.exp(scores - top).astype(BF16)
                    out = dot(terms, jnp.where(key_mine, values, BF16(1)))
                    total = pltpu.roll(out, HEAD_DIM, 1)
                    mixed.append(out / total)
                    log_total = top + jnp.log(jnp.where(mine, total, out))
                    cols = cols_ref[at, :]
                    cols_ref[at, :] = jnp.where(lane == first_head + i, log_total, cols)
                attn_ref[block, at, :] = jnp.where(lane < HEAD_DIM, mixed[0], mixed[1]).astype(BF16)
            return inner

        lax.fori_loop(0, 2, pair, 0)
        return carry

    lax.fori_loop(0, steps, step, 0)
    lse_ref[...] = cols_ref[...].T[: lse_ref.shape[0], :]

    def finish(tile, carry):
        at = pl.ds(tile * TILE, TILE)
        heads = jnp.concatenate([attn_ref[2 * p + y, at, :] for y in range(2) for p in range(3)], 1)
        branch = dot(heads, wo_ref[...])
        mean = jnp.sum(branch, axis=-1, keepdims=True) * (1.0 / width)
        mid_ref[at, :] = drop_last(x_ref[at, :].astype(F32) + branch - mean).astype(BF16)
        return carry

    lax.fori_loop(0, tiles, finish, 0)


def mlp_kernel(
    info_ref, mid_ref, og_ref, gain_ref, w1_ref, w2_ref,
    out_ref, dmid_ref, g1_ref, g2_ref, gg_ref,
    n2_ref, n2t_ref, d2_ref, d2t_ref, act_ref, dpre_ref, br_ref, dn_ref,
):
    rows, width = mid_ref.shape
    steps = w1_ref.shape[0]
    chunk = w1_ref.shape[2]
    tiles = rows // TILE
    live_count = info_ref[1]
    gain = gain_ref[...]

    def live_of(tile):
        row = tile * TILE + lax.broadcasted_iota(jnp.int32, (TILE, 1), 0)
        return (row < live_count).astype(F32)

    for tile in range(tiles):
        at = pl.ds(tile * TILE, TILE)
        fhat, _ = norm_parts(mid_ref[at, :].astype(F32))
        norm = (fhat * gain).astype(BF16)
        n2_ref[at, :] = norm
        n2t_ref[:, at] = norm.T
        out_live = drop_last(og_ref[at, :].astype(F32)) * live_of(tile)
        wide = widen(out_live).astype(BF16)
        d2_ref[at, :] = wide
        d2t_ref[:, at] = wide.T

    br_ref[...] = jnp.zeros_like(br_ref)
    dn_ref[...] = jnp.zeros_like(dn_ref)

    def step(p, carry):
        def rows_step(tile, inner):
            at = pl.ds(tile * TILE, TILE)
            norm = n2_ref[at, :]
            wide = d2_ref[at, :]
            br = br_ref[at, :]
            dn = dn_ref[at, :]
            for n in range(chunk // TILE):
                col = pl.ds(n * TILE, TILE)
                w1 = w1_ref[p, :, col]
                w2 = w2_ref[p, col, :]
                pre = dot(norm, w1)
                d_act = dot_rows(wide, w2)
                square = pre * pre
                inner_arg = (0.7978845608028654 * pre) * (1.0 + 0.044715 * square)
                tanh = jnp.tanh(inner_arg)
                half = 0.5 * (1.0 + tanh)
                act = (pre * half).astype(BF16)
                slope = half + (0.5 * pre) * (1.0 - tanh * tanh) * (
                    0.7978845608028654 + (3.0 * 0.044715 * 0.7978845608028654) * square
                )
                d_pre = (d_act * slope).astype(BF16)
                act_ref[at, col] = act
                dpre_ref[at, col] = d_pre
                br = br + dot(act, w2)
                dn = dn + dot_rows(d_pre, w1)
            br_ref[at, :] = br
            dn_ref[at, :] = dn
            return inner

        lax.fori_loop(0, tiles, rows_step, 0)

        def grad_step(tile, inner):
            at = pl.ds(tile * TILE, TILE)
            g2_ref[p, at, :] = dot(d2t_ref[at, :], act_ref[...]).astype(BF16)
            g1_ref[p, at, :] = dot(n2t_ref[at, :], dpre_ref[...]).astype(BF16)
            return inner

        lax.fori_loop(0, width // TILE, grad_step, 0)
        return carry

    lax.fori_loop(0, steps, step, 0)
    gg_ref[...] = jnp.zeros_like(gg_ref)

    def finish(tile, carry):
        at = pl.ds(tile * TILE, TILE)
        row = tile * TILE + lax.broadcasted_iota(jnp.int32, (TILE, 1), 0)
        live = (row < live_count).astype(F32)
        mid = mid_ref[at, :].astype(F32)
        branch = br_ref[at, :]
        mean = jnp.sum(branch, axis=-1, keepdims=True) * (1.0 / width)
        out_ref[at, :] = ((mid + branch - mean) * live).astype(BF16)
        fhat, scale = norm_parts(mid)
        grad = dn_ref[at, :]
        back = norm_back(fhat, scale, gain, grad)
        gg_ref[...] += jnp.sum((grad * fhat).reshape(TILE // 8, 8, width), axis=0)
        out_live = og_ref[at, :].astype(F32) * live
        dmid_ref[at, :] = drop_last(out_live + back).astype(BF16)
        return carry

    lax.fori_loop(0, tiles, finish, 0)


def back_kernel(
    info_ref, x_ref, dmid_ref, gain_ref, qkv_ref, attn_ref, lse_ref, w_ref, wo_ref,
    grad_ref, g0_ref, gg_ref,
    n1t_ref, attnt_ref, d1_ref, bias_ref, dn_ref, do_ref, dqt_ref, dqkv_ref,
):
    rows, width = x_ref.shape
    steps = w_ref.shape[0]
    tiles = rows // TILE
    length, live_count = info_ref[0], info_ref[1]
    gain = gain_ref[...]

    for tile in range(tiles):
        at = pl.ds(tile * TILE, TILE)
        fhat, _ = norm_parts(x_ref[at, :].astype(F32))
        n1t_ref[:, at] = (fhat * gain).astype(BF16).T
        d1_ref[at, :] = widen(drop_last(dmid_ref[at, :].astype(F32))).astype(BF16)
        for y in range(2):
            for p in range(3):
                lo = 384 * y + LANE * p
                attnt_ref[pl.ds(lo, LANE), at] = attn_ref[2 * p + y, at, :].T
        key = tile * TILE + lax.broadcasted_iota(jnp.int32, (TILE, rows), 0)
        query = lax.broadcasted_iota(jnp.int32, (TILE, rows), 1)
        bias_ref[at, :] = jnp.where(allowed_of(query, key, length, live_count), 0.0, MASKED_SCORE)

    dn_ref[...] = jnp.zeros_like(dn_ref)

    def step(p, carry):
        def project(tile, inner):
            at = pl.ds(tile * TILE, TILE)
            wo = jnp.concatenate([wo_ref[p], wo_ref[p + 3]], 0)
            out = dot_rows(d1_ref[at, :], wo).astype(BF16)
            do_ref[0, at, :] = out[:, :LANE]
            do_ref[1, at, :] = out[:, LANE:]
            return inner

        lax.fori_loop(0, tiles, project, 0)

        def pair(y, inner):
            block = 2 * p + y
            first_head = 6 * y + 2 * p
            product = (do_ref[y].astype(F32) * attn_ref[block].astype(F32)).T
            dots = [
                jnp.sum(product[i * HEAD_DIM : (i + 1) * HEAD_DIM, :], axis=0, keepdims=True)
                for i in range(2)
            ]
            lses = [lse_ref[pl.ds(first_head + i, 1), :] for i in range(2)]
            dqt_ref[...] = jnp.zeros_like(dqt_ref)
            for kb in range(tiles):
                lo = kb * TILE
                at = pl.ds(lo, TILE)
                rest = pl.ds(lo, rows - lo)
                lane = lane_of((TILE, LANE))
                query = qkv_ref[block, 0, rest, :] * BF16(HEAD_DIM**-0.5)
                keys = qkv_ref[block, 1, at, :]
                values = qkv_ref[block, 2, at, :]
                d_out = do_ref[y, rest, :]
                d_keys, d_values = [], []
                for i in range(2):
                    mine = (lane < HEAD_DIM) if i == 0 else (lane >= HEAD_DIM)
                    keys_mine = jnp.where(mine, keys, BF16(0))
                    scores = dot_rows(keys_mine, query) + bias_ref[at, rest]
                    probs = jnp.exp(scores - lses[i][:, lo:])
                    d_probs = dot_rows(jnp.where(mine, values, BF16(0)), d_out)
                    d_scores = (probs * (d_probs - dots[i][:, lo:])).astype(BF16)
                    d_values.append(dot(probs.astype(BF16), d_out))
                    d_keys.append(dot(d_scores, query))
                    dqt_ref[:, rest] += dot(keys_mine.T, d_scores)
                dqkv_ref[at, pl.ds(pl.multiple_of((2 + y) * LANE, LANE), LANE)] = jnp.where(
                    lane < HEAD_DIM, d_keys[0], d_keys[1]
                ).astype(BF16)
                dqkv_ref[at, pl.ds(pl.multiple_of((4 + y) * LANE, LANE), LANE)] = jnp.where(
                    lane < HEAD_DIM, d_values[0], d_values[1]
                ).astype(BF16)
            d_query = (dqt_ref[...] * HEAD_DIM**-0.5).T.astype(BF16)
            dqkv_ref[:, pl.ds(pl.multiple_of(y * LANE, LANE), LANE)] = d_query
            return inner

        lax.fori_loop(0, 2, pair, 0)

        def grads(tile, inner):
            at = pl.ds(tile * TILE, TILE)
            g0_ref[p, at, pl.ds(0, 6 * LANE)] = dot(n1t_ref[at, :], dqkv_ref[...]).astype(BF16)
            wide = jnp.concatenate(
                [
                    d1_ref[:, pl.ds(pl.multiple_of(384 * y + LANE * p, LANE), LANE)]
                    for y in range(2)
                ],
                1,
            )
            g0_ref[p, at, pl.ds(6 * LANE, 2 * LANE)] = dot(attnt_ref[at, :], wide).astype(BF16)
            return inner

        lax.fori_loop(0, width // TILE, grads, 0)

        def norm_grads(tile, inner):
            at = pl.ds(tile * TILE, TILE)
            dn_ref[at, :] += dot_rows(dqkv_ref[at, :], w_ref[p])
            return inner

        lax.fori_loop(0, tiles, norm_grads, 0)
        return carry

    lax.fori_loop(0, steps, step, 0)
    gg_ref[...] = jnp.zeros_like(gg_ref)

    def finish(tile, carry):
        at = pl.ds(tile * TILE, TILE)
        fhat, scale = norm_parts(x_ref[at, :].astype(F32))
        grad = dn_ref[at, :]
        back = norm_back(fhat, scale, gain, grad)
        gg_ref[...] += jnp.sum((grad * fhat).reshape(TILE // 8, 8, width), axis=0)
        grad_ref[at, :] = (dmid_ref[at, :].astype(F32) + back).astype(BF16)
        return carry

    lax.fori_loop(0, tiles, finish, 0)


def call(kernel, outs, scratch, count):
    in_vmem = pl.BlockSpec(memory_space=pltpu.VMEM)
    return pl.pallas_call(
        kernel,
        out_shape=[jax.ShapeDtypeStruct(*leaf) for leaf in outs],
        in_specs=[pl.BlockSpec(memory_space=pltpu.SMEM)] + [in_vmem] * (count - 1),
        out_specs=[in_vmem] * len(outs),
        scratch_shapes=[pltpu.VMEM(*leaf) for leaf in scratch],
        compiler_params=pltpu.CompilerParams(vmem_limit_bytes=VMEM_LIMIT),
    )


def chunked_columns(weight):
    width = weight.shape[0]
    groups = weight.shape[1] // (6 * LANE)
    split = weight.reshape(width, groups, 2, 3, LANE)
    return split.transpose(3, 0, 1, 2, 4).reshape(3, width, groups * 2 * LANE)


def unchunked_columns(chunks):
    width, columns = chunks.shape[1:]
    split = chunks.reshape(3, width, columns // (2 * LANE), 2, LANE)
    return split.transpose(1, 2, 3, 0, 4).reshape(width, 3 * columns)


def attention_forward(info, x, gain, w_in, w_out):
    rows, width = x.shape
    return call(
        attention_kernel,
        [
            ((6, 3, rows, LANE), BF16),
            ((6, rows, LANE), BF16),
            ((16, rows), F32),
            ((rows, width), BF16),
        ],
        [((rows, width), BF16), ((rows, rows), F32), ((rows, LANE), F32)],
        5,
    )(info, x, gain, w_in, w_out)


def mlp_both(info, mid, og, gain, w1, w2):
    rows, width = mid.shape
    chunk = w1.shape[2]
    return call(
        mlp_kernel,
        [
            ((rows, width), BF16),
            ((rows, width), BF16),
            ((3, width, chunk), BF16),
            ((3, width, chunk), BF16),
            ((8, width), F32),
        ],
        [
            ((rows, width), BF16),
            ((width, rows), BF16),
            ((rows, width), BF16),
            ((width, rows), BF16),
            ((rows, chunk), BF16),
            ((rows, chunk), BF16),
            ((rows, width), F32),
            ((rows, width), F32),
        ],
        6,
    )(info, mid, og, gain, w1, w2)


def attention_backward(info, x, dmid, gain, qkv, attn, lse, w_in, w_out):
    rows, width = x.shape
    return call(
        back_kernel,
        [((rows, width), BF16), ((3, width, 8 * LANE), BF16), ((8, width), F32)],
        [
            ((width, rows), BF16),
            ((width, rows), BF16),
            ((rows, width), BF16),
            ((rows, rows), F32),
            ((rows, width), F32),
            ((2, rows, LANE), BF16),
            ((LANE, rows), F32),
            ((rows, 6 * LANE), BF16),
        ],
        9,
    )(info, x, dmid, gain, qkv, attn, lse, w_in, w_out)


def swap_section(value):
    return lax.ppermute(value, "section", [(0, 1), (1, 0)])


def per_device(stream_in, seq_len, live_rows, norm_gain, first_weight, down_weight, out_grad):
    section = lax.axis_index("section")
    rows = stream_in.shape[0]
    width = norm_gain.shape[1]
    info = jnp.stack([seq_len[0], live_rows[0] - section * rows])
    first = section == 0
    other_weight = swap_section(first_weight[0])
    other_down = swap_section(down_weight)
    gains = lax.all_gather(norm_gain[0], "section")
    w0 = jnp.where(first, first_weight[0], other_weight)
    w1 = jnp.where(first, other_weight, first_weight[0])
    down = jnp.concatenate(
        [jnp.where(first, down_weight, other_down), jnp.where(first, other_down, down_weight)], 0
    )
    x = jnp.pad(stream_in, ((0, 0), (0, 1)))
    og = jnp.pad(out_grad, ((0, 0), (0, 1)))
    w_in = chunked_columns(w0[:, : 3 * width])
    w_out = w0[:, 3 * width :]
    w1c = chunked_columns(w1)
    w2c = chunked_columns(down.T).transpose(0, 2, 1)
    qkv, attn, lse, mid = attention_forward(info, x, gains[0:1], w_in, w_out)
    out, dmid, g1, g2, gg1 = mlp_both(info, mid, og, gains[1:2], w1c, w2c)
    grad, g0, gg0 = attention_backward(
        info, x, dmid, gains[0:1], qkv, attn, lse, w_in, w_out.reshape(6, LANE, width)
    )
    first_sum = jnp.stack([unchunked_columns(g0), unchunked_columns(g1)])
    first_out = lax.psum_scatter(first_sum, "section", scatter_dimension=0, tiled=True)
    first_out = lax.psum_scatter(first_out, "dp", scatter_dimension=2, tiled=True)
    down_sum = unchunked_columns(g2).T
    down_out = lax.psum_scatter(down_sum, "section", scatter_dimension=0, tiled=True)
    down_out = lax.psum_scatter(down_out, "dp", scatter_dimension=1, tiled=True)
    gain_sum = jnp.stack([jnp.sum(gg0, 0), jnp.sum(gg1, 0)])
    gain_out = lax.psum_scatter(gain_sum, "section", scatter_dimension=0, tiled=True)
    gain_out = lax.psum_scatter(gain_out, "dp", scatter_dimension=1, tiled=True)
    return (
        out[:, : width - 1],
        grad[:, : width - 1],
        gain_out,
        first_out.astype(F32),
        down_out.astype(F32),
    )


def solution(mesh):
    in_specs = (
        P(("dp", "section"), None),
        P("dp"),
        P("dp"),
        P("section", None),
        P("section", None, None),
        P("section", None),
        P(("dp", "section"), None),
    )
    out_specs = (
        P(("dp", "section"), None),
        P(("dp", "section"), None),
        P("section", "dp"),
        P("section", None, "dp"),
        P("section", "dp"),
    )
    return jax.shard_map(
        per_device, mesh=mesh, in_specs=in_specs, out_specs=out_specs, check_vma=False
    )
```

```python
import functools

import jax
import jax.numpy as jnp
from jax import lax
from jax.experimental import pallas as pl
from jax.experimental.pallas import tpu as pltpu
from jax.sharding import PartitionSpec as P

HEADS = 12
HEAD_DIM = 64
EPSILON = 1e-05
MASKED_SCORE = -1e30
LANE = 128
TILE = 256
F32 = jnp.float32
BF16 = jnp.bfloat16
VMEM_LIMIT = 66000000


def dot(left, right):
    return lax.dot_general(left, right, (((1,), (0,)), ((), ())), preferred_element_type=F32)


def dot_rows(left, right):
    return lax.dot_general(left, right, (((1,), (1,)), ((), ())), preferred_element_type=F32)


def dot_cols(left, right):
    return lax.dot_general(left, right, (((0,), (0,)), ((), ())), preferred_element_type=F32)


def lane_of(shape):
    return lax.broadcasted_iota(jnp.int32, shape, 1)


def padded(block):
    return jnp.pad(block.astype(F32), ((0, 0), (0, 1)))


def full_width(block):
    lane = lane_of(block.shape)
    last = block.shape[1] - 1
    kept = jnp.where(lane == last, 0.0, block)
    return jnp.where(lane == last, -jnp.sum(kept, axis=-1, keepdims=True), kept)


def norm_parts(block):
    full = full_width(block)
    scale = lax.rsqrt(jnp.mean(full * full, axis=-1, keepdims=True) + EPSILON)
    return full * scale, scale


def norm_back(fhat, scale, gain, grad):
    weighted = grad * gain
    inner = jnp.mean(weighted * fhat, axis=-1, keepdims=True)
    error = scale * (weighted - fhat * inner)
    last = error.shape[1] - 1
    tail = jnp.sum(jnp.where(lane_of(error.shape) == last, error, 0.0), axis=-1, keepdims=True)
    return error - tail


def drop_last(block):
    return jnp.where(lane_of(block.shape) == block.shape[1] - 1, 0.0, block)


def widen(block):
    return block - jnp.sum(block, axis=-1, keepdims=True) * (1.0 / block.shape[1])


def allowed_of(query_pos, key_pos, length, live_count):
    start = query_pos & (-length)
    usable = (key_pos < live_count) | (key_pos == query_pos)
    return (key_pos >= start) & (key_pos <= query_pos) & usable


MESH = pl.DeviceIdType.MESH
HALF = 384
PART = 192
GROUP = 48


class Refs:
    def __init__(self, **refs):
        self.__dict__.update(refs)


def scratch_of(rows, width, reduce):
    vmem = pltpu.VMEM
    dma = pltpu.SemaphoreType.DMA
    credit = pltpu.SemaphoreType.REGULAR
    shapes = dict(
        xs=vmem((rows, width - 1), BF16),
        ogs=vmem((rows, width - 1), BF16),
        wbuf=vmem((2, 4, width, width), BF16),
        w2=vmem((3, 8, LANE, width), BF16),
        gains=vmem((2, 1, width), F32),
        qkv=vmem((6, 3, rows, LANE), BF16),
        attnt=vmem((width, rows), BF16),
        mid=vmem((rows, width), BF16),
        nrm=vmem((rows, width), BF16),
        wide=vmem((rows, width), BF16),
        nt=vmem((width, rows), BF16),
        wt=vmem((width, rows), BF16),
        act=vmem((rows, 8 * LANE), BF16),
        dpre=vmem((rows, 8 * LANE), BF16),
        br=vmem((rows, width), F32),
        dn=vmem((rows, width), F32),
        bias=vmem((rows, rows), BF16),
        vt=vmem((LANE, rows), BF16),
        lse=vmem((16, rows), F32),
        do=vmem((2, rows, LANE), BF16),
        dqt=vmem((LANE, rows), F32),
        gg=vmem((2, 8, width), F32),
        gbig=vmem((8, width, LANE), BF16),
        gdown=vmem((8, width, LANE), BF16),
        load_sem=dma((10,)),
        out_sem=dma((5,)),
        ga_send=dma((4, 11)),
        ga_recv=dma((4, 11)),
    )
    if reduce:
        shapes.update(
            g_rc=vmem((8, HALF, LANE), BF16),
            g_keep=vmem((4, HALF, LANE), BF16),
            g_s1=vmem((4, HALF, LANE), BF16),
            g_r2=vmem((2, 4, HALF, LANE), BF16),
            g_s2=vmem((3, HALF, LANE), BF16),
            g_own=vmem((HALF, LANE), BF16),
            g_rz=vmem((2, 3, HALF, LANE), BF16),
            g_sx=vmem((HALF, LANE), BF16),
            g_rx=vmem((3, HALF, LANE), BF16),
            g_acc=vmem((3, width, LANE), F32),
            d_rc=vmem((8, HALF, LANE), BF16),
            d_keep=vmem((4, HALF, LANE), BF16),
            d_s1=vmem((4, HALF, LANE), BF16),
            d_r2=vmem((2, 4, HALF, LANE), BF16),
            d_keep2=vmem((4, PART, LANE), BF16),
            d_s2=vmem((4, PART, LANE), BF16),
            d_ry=vmem((2, 4, PART, LANE), BF16),
            d_s3=vmem((3, 4, GROUP, LANE), BF16),
            d_own=vmem((4, GROUP, LANE), BF16),
            d_rz=vmem((2, 3, 4, GROUP, LANE), BF16),
            d_acc=vmem((3, 4, GROUP, LANE), F32),
            n_sum=vmem((8, width), F32),
            n_send=vmem((4, 8, width), F32),
            n_recv=vmem((6, 8, width), F32),
            core_sem=dma((2, 2)),
            gy_send=dma((4,)),
            gy_recv=dma((2, 4)),
            gz_send=dma((3,)),
            gz_recv=dma((2, 3)),
            x_sem=dma((4,)),
            dx_sem=dma((3,)),
            dy_sem=dma((3,)),
            dz_send=dma((3,)),
            dz_recv=dma((2, 3)),
            n_sem=dma((2, 6)),
            end_sem=dma((2, 3)),
            credit=credit((6,)),
            z_credit=credit((2, 3)),
        )
    return shapes


class Place:
    def __init__(self):
        self.dp = lax.axis_index("dp")
        self.section = lax.axis_index("section")
        self.core = self.dp % 2
        self.y = (self.dp // 2) % 2
        self.z = self.dp // 4
        self.unit = self.dp % 4
        self.core_id = {"dp": self.dp + 1 - 2 * self.core}
        self.y_id = {"dp": self.dp + 2 - 4 * self.y}
        self.x_id = {"section": 1 - self.section}

    def z_of(self, r):
        return (self.z + r) % 4

    def z_back(self, r):
        return (self.z + 4 - r) % 4

    def z_id(self, r):
        return {"dp": self.dp + 4 * (self.z_of(r) - self.z)}

    def z_back_id(self, r):
        return {"dp": self.dp + 4 * (self.z_back(r) - self.z)}


def remote(source, target, send_sem, recv_sem, device):
    return pltpu.make_async_remote_copy(
        src_ref=source, dst_ref=target, send_sem=send_sem, recv_sem=recv_sem,
        device_id=device, device_id_type=MESH,
    )


def landed(target, send_sem, recv_sem, device):
    remote(target, target, send_sem, recv_sem, device).wait_recv()


def sent(source, send_sem, recv_sem, device):
    remote(source, source, send_sem, recv_sem, device).wait_send()


class Gather:
    def __init__(self, refs, place):
        self.refs, self.place = refs, place
        self.mine, self.theirs = place.section, 1 - place.section

    def block(self, slot, piece, unit):
        kind, k = piece
        if kind == "down":
            return self.refs.w2.at[k, 4 * slot + unit], k + 7
        if kind == "start":
            size = PART // 2
            rows = pl.ds(pl.multiple_of(PART * unit + size * (k % 2), size), size)
            return self.refs.wbuf.at[slot, 0, rows, pl.ds(HALF * (k // 2), HALF)], k
        rows = pl.ds(pl.multiple_of(PART * unit, PART), PART)
        return self.refs.wbuf.at[slot, k, rows, :], k + 3

    def copy(self, kind, piece, slot, unit, device):
        ref, at = self.block(slot, piece, unit)
        return remote(ref, ref, self.refs.ga_send.at[kind, at], self.refs.ga_recv.at[kind, at], device)

    def send_x(self, piece):
        self.copy(0, piece, self.mine, self.place.unit, self.place.x_id).start()

    def forward(self, piece):
        place = self.place
        self.copy(0, piece, self.theirs, place.unit, place.x_id).wait_recv()
        self.copy(2, piece, self.theirs, place.unit, place.y_id).start()
        self.copy(1, piece, self.theirs, place.unit, place.core_id).start()

    def relay(self, piece):
        place = self.place
        other = (place.unit + 2) % 4
        self.copy(2, piece, self.theirs, other, place.y_id).wait_recv()
        self.copy(3, piece, self.theirs, other, place.core_id).start()

    def use(self, piece):
        place = self.place
        beside = place.unit + 1 - 2 * place.core
        self.copy(1, piece, self.theirs, beside, place.core_id).wait_recv()
        self.copy(3, piece, self.theirs, (beside + 2) % 4, place.core_id).wait_recv()

    def drain(self, piece):
        place = self.place
        self.copy(0, piece, self.mine, place.unit, place.x_id).wait_send()
        self.copy(1, piece, self.theirs, place.unit, place.core_id).wait_send()
        self.copy(2, piece, self.theirs, place.unit, place.y_id).wait_send()
        self.copy(3, piece, self.theirs, (place.unit + 2) % 4, place.core_id).wait_send()


START = [("start", k) for k in range(4)]
FIRST = [("first", k) for k in range(1, 4)]
DOWN = [("down", k) for k in range(3)]


def half_rows(half):
    return pl.ds(pl.multiple_of(HALF * half, HALF), HALF)


def when(condition, action):
    if isinstance(condition, bool):
        if condition:
            action()
    else:
        pl.when(condition)(action)


class BigSum:
    jobs = 6

    def __init__(self, refs, place):
        self.r, self.p = refs, place

    def core_copy(self):
        r, p = self.r, self.p
        return remote(
            r.gbig.at[:, half_rows(1 - p.core), :], r.g_rc, r.core_sem.at[0, 0], r.core_sem.at[1, 0], p.core_id
        )

    def start(self, j):
        when(j >= 1, lambda: pl.semaphore_wait(self.r.credit.at[0], 1))
        self.core_copy().start()

    def y_copy(self, j, block):
        r, p = self.r, self.p
        return remote(
            r.g_s1.at[block], r.g_r2.at[j % 2, block], r.gy_send.at[block], r.gy_recv.at[j % 2, block], p.y_id
        )

    def after_core(self, j):
        r, p = self.r, self.p
        self.core_copy().wait()
        own = half_rows(p.core)
        when(j >= 2, lambda: pl.semaphore_wait(r.credit.at[1], 1))
        for k in range(4):
            z = p.z_of((k + 1) % 4)
            at = 4 * (1 - p.y) + z
            r.g_s1[z] = r.gbig[at, own, :] + r.g_rc[at]
            self.y_copy(j, z).start()
        for z in range(4):
            at = 4 * p.y + z
            r.g_keep[z] = r.gbig[at, own, :] + r.g_rc[at]
        when(
            j <= self.jobs - 2,
            lambda: pl.semaphore_signal(r.credit.at[0], inc=1, device_id=p.core_id, device_id_type=MESH),
        )

    def z_copy(self, j, k):
        r, p = self.r, self.p
        return remote(
            r.g_s2.at[k - 1], r.g_rz.at[j % 2, k - 1], r.gz_send.at[k - 1], r.gz_recv.at[j % 2, k - 1], p.z_id(k)
        )

    def after_y(self, j):
        r, p = self.r, self.p
        slot = j % 2
        for k in range(1, 4):
            z = p.z_of(k)
            self.y_copy(j, z).wait_recv()
            r.g_s2[k - 1] = r.g_keep[z] + r.g_r2[slot, z]
            when(j >= 2, lambda k=k: pl.semaphore_wait(r.z_credit.at[0, k - 1], 1))
            self.z_copy(j, k).start()
        self.y_copy(j, p.z).wait_recv()
        r.g_own[...] = r.g_keep[p.z] + r.g_r2[slot, p.z]
        for k in range(4):
            self.y_copy(j, k).wait_send()
        when(
            j <= self.jobs - 3,
            lambda: pl.semaphore_signal(r.credit.at[1], inc=1, device_id=p.y_id, device_id_type=MESH),
        )

    def x_copy(self, chunk):
        r, p = self.r, self.p
        return remote(r.g_sx, r.g_rx.at[chunk], r.x_sem.at[3], r.x_sem.at[chunk], p.x_id)

    def after_z(self, j, chunk, target):
        r, p = self.r, self.p
        slot = j % 2
        for k in range(1, 4):
            self.z_copy(j, k).wait()
        total = r.g_own[...].astype(F32)
        for k in range(3):
            total = total + r.g_rz[slot, k].astype(F32)

        @pl.when(p.section != target)
        def _():
            r.g_sx[...] = total.astype(BF16)
            self.x_copy(chunk).start()

        @pl.when(p.section == target)
        def _():
            r.g_acc[chunk, half_rows(p.core), :] = total

        for k in range(1, 4):
            when(
                j <= self.jobs - 3,
                lambda k=k: pl.semaphore_signal(
                    r.z_credit.at[0, k - 1], inc=1, device_id=p.z_back_id(k), device_id_type=MESH
                ),
            )

    def after_x(self, chunk, target):
        r, p = self.r, self.p

        @pl.when(p.section != target)
        def _():
            self.x_copy(chunk).wait_send()

        @pl.when(p.section == target)
        def _():
            self.x_copy(chunk).wait_recv()
            own = half_rows(p.core)
            r.g_acc[chunk, own, :] = r.g_acc[chunk, own, :] + r.g_rx[chunk].astype(F32)


class DownSum:
    jobs = 3

    def __init__(self, refs, place):
        self.r, self.p = refs, place

    def core_copy(self):
        r, p = self.r, self.p
        return remote(
            r.gdown.at[:, half_rows(1 - p.core), :], r.d_rc, r.core_sem.at[0, 1], r.core_sem.at[1, 1], p.core_id
        )

    def start(self, j):
        when(j >= 1, lambda: pl.semaphore_wait(self.r.credit.at[2], 1))
        self.core_copy().start()

    def x_copy(self, j):
        r, p = self.r, self.p
        return remote(r.d_s1, r.d_r2.at[j % 2], r.dx_sem.at[2], r.dx_sem.at[j % 2], p.x_id)

    def after_core(self, j):
        r, p = self.r, self.p
        self.core_copy().wait()
        own = half_rows(p.core)
        for k in range(4):
            at = 4 * (1 - p.section) + k
            r.d_s1[k] = r.gdown[at, own, :] + r.d_rc[at]
        when(j >= 2, lambda: pl.semaphore_wait(r.credit.at[3], 1))
        self.x_copy(j).start()
        for k in range(4):
            at = 4 * p.section + k
            r.d_keep[k] = r.gdown[at, own, :] + r.d_rc[at]
        when(
            j <= self.jobs - 2,
            lambda: pl.semaphore_signal(r.credit.at[2], inc=1, device_id=p.core_id, device_id_type=MESH),
        )

    def y_copy(self, j):
        r, p = self.r, self.p
        return remote(r.d_s2, r.d_ry.at[j % 2], r.dy_sem.at[2], r.dy_sem.at[j % 2], p.y_id)

    def after_x(self, j):
        r, p = self.r, self.p
        slot = j % 2
        self.x_copy(j).wait()
        theirs = pl.ds(pl.multiple_of(PART * (1 - p.y), PART), PART)
        mine = pl.ds(pl.multiple_of(PART * p.y, PART), PART)
        for k in range(4):
            r.d_s2[k] = r.d_keep[k, theirs, :] + r.d_r2[slot, k, theirs, :]
        when(j >= 2, lambda: pl.semaphore_wait(r.credit.at[4], 1))
        self.y_copy(j).start()
        for k in range(4):
            r.d_keep2[k] = r.d_keep[k, mine, :] + r.d_r2[slot, k, mine, :]
        when(
            j <= self.jobs - 3,
            lambda: pl.semaphore_signal(r.credit.at[3], inc=1, device_id=p.x_id, device_id_type=MESH),
        )

    def z_copy(self, j, k):
        r, p = self.r, self.p
        return remote(
            r.d_s3.at[k - 1], r.d_rz.at[j % 2, k - 1], r.dz_send.at[k - 1], r.dz_recv.at[j % 2, k - 1], p.z_id(k)
        )

    def after_y(self, j):
        r, p = self.r, self.p
        slot = j % 2
        self.y_copy(j).wait()
        for k in range(4):
            rows = pl.ds(pl.multiple_of(GROUP * p.z_of(k), GROUP), GROUP)
            for f in range(4):
                total = r.d_keep2[f, rows, :] + r.d_ry[slot, f, rows, :]
                if k == 0:
                    r.d_own[f] = total
                else:
                    r.d_s3[k - 1, f] = total
        for k in range(1, 4):
            when(j >= 2, lambda k=k: pl.semaphore_wait(r.z_credit.at[1, k - 1], 1))
            self.z_copy(j, k).start()
        when(
            j <= self.jobs - 3,
            lambda: pl.semaphore_signal(r.credit.at[4], inc=1, device_id=p.y_id, device_id_type=MESH),
        )

    def after_z(self, j):
        r, p = self.r, self.p
        slot = j % 2
        for k in range(1, 4):
            self.z_copy(j, k).wait()
        for f in range(4):
            total = r.d_own[f].astype(F32)
            for k in range(3):
                total = total + r.d_rz[slot, k, f].astype(F32)
            r.d_acc[j, f] = total
        for k in range(1, 4):
            when(
                j <= self.jobs - 3,
                lambda k=k: pl.semaphore_signal(
                    r.z_credit.at[1, k - 1], inc=1, device_id=p.z_back_id(k), device_id_type=MESH
                ),
            )


class NormSum:
    def __init__(self, refs, place):
        self.r, self.p = refs, place

    def copy(self, stage, slot, device):
        r = self.r
        return remote(
            r.n_send.at[stage], r.n_recv.at[slot], r.n_sem.at[0, slot], r.n_sem.at[1, slot], device
        )

    def routes(self, stage):
        p = self.p
        return [
            [(0, p.core_id)], [(1, p.y_id)], [(2, p.z_id(1)), (3, p.z_id(2)), (4, p.z_id(3))], [(5, p.x_id)]
        ][stage]

    def send(self, stage):
        r = self.r
        r.n_send[stage] = r.n_sum[...]
        for slot, device in self.routes(stage):
            self.copy(stage, slot, device).start()

    def receive(self, stage):
        r = self.r
        for slot, device in self.routes(stage):
            self.copy(stage, slot, device).wait()
            r.n_sum[...] += r.n_recv[slot]


def layer_kernel(reduce, names, length_ref, live_ref, x_hbm, og_hbm, gain_in, first_hbm, down_hbm, out_hbm, grad_hbm, *rest):
    outs = rest[:3]
    r = Refs(**dict(zip(names, rest[3:])))
    place = Place()
    rows, width = r.mid.shape
    tiles = rows // TILE
    section = place.section
    length, live_count = length_ref[0], live_ref[0] - section * rows
    gather = Gather(r, place)
    big, down, norms = BigSum(r, place), DownSum(r, place), NormSum(r, place)

    def tile_at(tile):
        return pl.ds(pl.multiple_of(tile * TILE, TILE), TILE)

    def wide_at(tile):
        return pl.ds(pl.multiple_of(tile * 2 * TILE, 2 * TILE), 2 * TILE)

    def lane_at(lo):
        return pl.ds(pl.multiple_of(lo, LANE), LANE)

    def load(source, target, index):
        return pltpu.make_async_copy(source, target, r.load_sem.at[index])

    barrier = pltpu.get_barrier_semaphore()
    greeted = [place.core_id, place.y_id, place.x_id]
    if reduce:
        greeted += [place.z_id(k) for k in range(1, 4)]
    for device in greeted:
        pl.semaphore_signal(barrier, inc=1, device_id=device, device_id_type=MESH)
    x_load = load(x_hbm, r.xs, 7)
    og_load = load(og_hbm, r.ogs, 8)
    gain_load = load(gain_in, r.gains.at[section], 9)
    gain_load.start()
    for k in range(3):
        for z in range(3):
            for y in range(2):
                lo = width * z + HALF * y + LANE * k
                load(
                    first_hbm.at[:, pl.ds(lo, LANE)],
                    r.wbuf.at[section, k, :, pl.ds((3 * y + z) * LANE, LANE)],
                    k,
                ).start()
        if k == 0:
            x_load.start()
    load(first_hbm.at[:, pl.ds(3 * width, width)], r.wbuf.at[section, 3], 3).start()
    og_load.start()
    for k in range(3):
        for z in range(2):
            for y in range(2):
                lo = width * z + HALF * y + LANE * k
                load(
                    down_hbm.at[pl.ds(lo, LANE), :], r.w2.at[k, 4 * section + 2 * z + y], 4 + k
                ).start()

    gain_load.wait()
    pl.semaphore_wait(barrier, len(greeted))

    gain_ref = r.gains.at[section]
    gain_copy = remote(gain_ref, gain_ref, r.ga_send.at[0, 10], r.ga_recv.at[0, 10], place.x_id)
    gain_copy.start()
    for k in range(4):
        load(r.wbuf.at[section, k], r.wbuf.at[section, k], k).wait()
        for piece in START if k == 0 else [("first", k)]:
            gather.send_x(piece)
    for k in range(3):
        mine = r.w2.at[k, pl.ds(4 * section, 4)]
        load(mine, mine, 4 + k).wait()
        gather.send_x(("down", k))
    og_load.wait()

    def live_of(tile):
        row = tile * TILE + lax.broadcasted_iota(jnp.int32, (TILE, 1), 0)
        return (row < live_count).astype(F32)

    for tile in range(tiles):
        at = tile_at(tile)
        out_live = padded(r.ogs[at, :]) * live_of(tile)
        wide = widen(out_live).astype(BF16)
        r.wide[at, :] = wide
        turned = wide.T
        if reduce:
            for z in range(4):
                for y in range(2):
                    for c in range(2):
                        lo = PART * z + 2 * GROUP * y + GROUP * c
                        to = HALF * c + PART * y + GROUP * z
                        r.wt[pl.ds(to, GROUP), at] = turned[lo : lo + GROUP, :]
        else:
            r.wt[:, at] = turned

    x_load.wait()
    theirs = r.gains.at[1 - section]
    landed(theirs, r.ga_send.at[0, 10], r.ga_recv.at[0, 10], place.x_id)

    def begin_step(tile, carry):
        at = tile_at(tile)
        fhat, _ = norm_parts(padded(r.xs[at, :]))
        r.nrm[at, :] = (fhat * r.gains[0]).astype(BF16)
        key = tile * TILE + lax.broadcasted_iota(jnp.int32, (TILE, rows), 0)
        query = lax.broadcasted_iota(jnp.int32, (TILE, rows), 1)
        allowed = allowed_of(query, key, length, live_count)
        r.bias[at, :] = jnp.where(allowed, 0.0, MASKED_SCORE).astype(BF16)
        return carry

    lax.fori_loop(0, tiles, begin_step, 0)
    gather.forward(START[0])
    gather.forward(START[1])
    gather.relay(START[0])
    gather.forward(START[2])
    gather.relay(START[1])
    gather.forward(START[3])

    def project_half(y):
        lanes = pl.ds(HALF * y, HALF)

        @pl.when(section == 1)
        def _():
            gather.use(START[2 * y])
            gather.use(START[2 * y + 1])

        def project(tile, inner):
            at = wide_at(tile)
            out = dot(r.nrm[at, :], r.wbuf[0, 0, :, lanes]).astype(BF16)
            for t in range(3):
                r.qkv[y, t, at, :] = out[:, t * LANE : (t + 1) * LANE]
            return inner

        lax.fori_loop(0, tiles // 2, project, 0)

    def attention_step(p, carry):
        def project(tile, inner):
            at = wide_at(tile)
            out = dot(r.nrm[at, :], r.wbuf[0, p]).astype(BF16)
            for t in range(3):
                for y in range(2):
                    lo = (3 * y + t) * LANE
                    r.qkv[2 * p + y, t, at, :] = out[:, lo : lo + LANE]
            return inner

        @pl.when(p >= 1)
        def _():
            lax.fori_loop(0, tiles // 2, project, 0)

        def pair(y, inner):
            block = 2 * p + y
            first_head = 6 * y + 2 * p

            turn = 2 * p + y

            @pl.when(turn == 0)
            def _():
                project_half(0)
                gather.relay(START[2])
                gather.relay(START[3])
                gather.forward(("first", 1))

            @pl.when(turn == 1)
            def _():
                project_half(1)
                gather.forward(("first", 2))

            @pl.when(turn == 2)
            def _():
                gather.forward(("first", 3))

            @pl.when(turn == 3)
            def _():
                gather.relay(("first", 2))

            @pl.when(turn == 4)
            def _():
                gather.relay(("first", 3))
                gather.forward(("down", 0))

            @pl.when(turn == 5)
            def _():
                gather.forward(("down", 1))
                gather.forward(("down", 2))

            r.vt[...] = r.qkv[block, 2].T
            out_rows = pl.multiple_of(HALF * y + LANE * p, LANE)

            def scores_of(qb, i):
                count = (qb + 1) * TILE
                at = pl.ds(qb * TILE, TILE)
                lane = lane_of((TILE, LANE))
                mine = (lane < HEAD_DIM) if i == 0 else (lane >= HEAD_DIM)
                query = jnp.where(mine, r.qkv[block, 0, at, :] * BF16(HEAD_DIM**-0.5), BF16(0))
                keys = r.qkv[block, 1, pl.ds(0, count), :]
                return dot_rows(keys, query) + r.bias[pl.ds(0, count), at].astype(F32)

            def mix(qb, i, scores):
                count = (qb + 1) * TILE
                at = pl.ds(qb * TILE, TILE)
                top = jnp.max(scores, axis=0, keepdims=True)
                terms = jnp.exp(scores - top).astype(BF16)
                values = jnp.concatenate(
                    [r.vt[pl.ds(i * HEAD_DIM, HEAD_DIM), pl.ds(0, count)], jnp.ones((16, count), BF16)], 0
                )
                out = dot(values, terms)
                total = out[HEAD_DIM : HEAD_DIM + 1, :]
                r.lse[pl.ds(first_head + i, 1), at] = top + jnp.log(total)
                r.attnt[pl.ds(out_rows + i * HEAD_DIM, HEAD_DIM), at] = (
                    out[:HEAD_DIM, :] / total
                ).astype(BF16)

            waiting = None
            for qb in range(tiles):
                for i in range(2):
                    scores = scores_of(qb, i)
                    if waiting is not None:
                        mix(*waiting)
                    waiting = (qb, i, scores)
            mix(*waiting)
            return inner

        lax.fori_loop(0, 2, pair, 0)
        pl.when(p == 0)(lambda: gather.relay(("first", 1)))
        pl.when(section == 1)(lambda: gather.use(("first", p + 1)))
        return carry

    lax.fori_loop(0, 3, attention_step, 0)

    gather.relay(("down", 0))

    def attention_end(tile, carry):
        at = tile_at(tile)
        branch = dot_cols(r.attnt[:, at], r.wbuf[0, 3])
        mean = jnp.sum(branch, axis=-1, keepdims=True) * (1.0 / width)
        mid = drop_last(padded(r.xs[at, :]) + branch - mean).astype(BF16)
        r.mid[at, :] = mid
        fhat, _ = norm_parts(mid.astype(F32))
        norm = (fhat * r.gains[1]).astype(BF16)
        r.nrm[at, :] = norm
        r.nt[:, at] = norm.T
        return carry

    for tile in range(tiles):
        attention_end(tile, 0)

    gather.relay(("down", 1))

    @pl.when(section == 0)
    def _():
        for piece in START + FIRST:
            gather.use(piece)

    r.br[...] = jnp.zeros_like(r.br)
    r.dn[...] = jnp.zeros_like(r.dn)

    def dump(source, output, chunk, index):
        copy = pltpu.make_async_copy(source, output.at[chunk], r.out_sem.at[index])
        copy.start()
        copy.wait()

    def mlp_step(p, carry):
        gather.use(("down", p))
        pl.when(p == 0)(lambda: gather.relay(("down", 2)))

        def first_columns(n):
            if n < 3:
                return jnp.concatenate(
                    [r.wbuf[1, p, :, pl.ds((3 * y + n) * LANE, LANE)] for y in range(2)], 1
                )
            return jnp.concatenate(
                [r.wbuf[1, 3, :, lane_at(HALF * y + LANE * p)] for y in range(2)], 1
            )

        def hidden(tile, n):
            at = tile_at(tile)
            col = pl.ds(n * TILE, TILE)
            pre = dot(r.nrm[at, :], first_columns(n))
            d_act = dot_rows(r.wide[at, :], r.w2[p, pl.ds(2 * n, 2)].reshape(TILE, width))
            square = pre * pre
            inner_arg = pre * (0.7978845608028654 + (0.044715 * 0.7978845608028654) * square)
            tanh = jnp.tanh(inner_arg)
            half = 0.5 + 0.5 * tanh
            slope = half + (0.5 * pre) * (1.0 - tanh * tanh) * (
                0.7978845608028654 + (3.0 * 0.044715 * 0.7978845608028654) * square
            )
            r.act[at, col] = (pre * half).astype(BF16)
            r.dpre[at, col] = (d_act * slope).astype(BF16)

        def branch_part(tile, m):
            at = tile_at(tile)
            col = pl.ds(m * TILE, TILE)
            w2 = r.w2[p, :, :, col].reshape(8 * LANE, TILE)
            r.br[at, col] += dot(r.act[at, :], w2)

        def norm_part(tile, m):
            at = tile_at(tile)
            col = pl.ds(m * TILE, TILE)
            w1 = jnp.concatenate(
                [
                    r.wbuf[1, p, col, pl.ds((3 * y + z) * LANE, LANE)]
                    for z in range(3)
                    for y in range(2)
                ]
                + [r.wbuf[1, 3, col, lane_at(HALF * y + LANE * p)] for y in range(2)],
                1,
            )
            r.dn[at, col] += dot_rows(r.dpre[at, :], w1)

        for n in range(4):
            hidden(0, n)

        def rows_step(tile, inner):
            for n in range(4):
                hidden(tile, n)
                if n < 3:
                    branch_part(tile - 1, n)
                    norm_part(tile - 1, n)
            return inner

        lax.fori_loop(1, tiles, rows_step, 0)
        for n in range(3):
            branch_part(tiles - 1, n)
            norm_part(tiles - 1, n)

        def grads(half):
            own = half_rows(half)
            for n in range(4):
                g1 = dot(r.nt[own, :], r.dpre[:, pl.ds(n * TILE, TILE)]).astype(BF16)
                for y in range(2):
                    r.gbig[4 * y + n, own, :] = g1[:, y * LANE : (y + 1) * LANE]

        def down_grads(half):
            own = half_rows(half)
            for n in range(4):
                g2 = dot(r.wt[own, :], r.act[:, pl.ds(n * TILE, TILE)]).astype(BF16)
                for y in range(2):
                    r.gdown[2 * n + y, own, :] = g2[:, y * LANE : (y + 1) * LANE]

        def half_step(step, inner):
            if not reduce:
                grads(step)
                down_grads(step)
                return inner
            half = (1 - place.core) * (1 - step) + place.core * step
            grads(half)
            pl.when(step == 0)(lambda: big.start(p))
            down_grads(half)
            pl.when(step == 0)(lambda: down.start(p))
            return inner

        lax.fori_loop(0, 2, half_step, 0)
        if reduce:

            @pl.when(p == 2)
            def _():
                big.after_z(0, 0, 1)
                down.after_y(0)

            @pl.when(p >= 1)
            def _():
                big.after_y(p - 1)
                down.after_x(p - 1)

            big.after_core(p)
            down.after_core(p)
        if not reduce:
            dump(r.gbig, outs[1], p, 0)
            dump(r.gdown, outs[2], p, 1)
        return carry

    lax.fori_loop(0, 3, mlp_step, 0)
    r.gg[...] = jnp.zeros_like(r.gg)

    def mlp_end(tile, carry):
        at = tile_at(tile)
        live = live_of(tile)
        mid = r.mid[at, :].astype(F32)
        out_live = padded(r.ogs[at, :]) * live
        branch = r.br[at, :]
        mean = jnp.sum(branch, axis=-1, keepdims=True) * (1.0 / width)
        out = ((mid + branch - mean) * live).astype(BF16)
        r.ogs[at, :] = out[:, : width - 1]
        fhat, scale = norm_parts(mid)
        grad = r.dn[at, :]
        back = norm_back(fhat, scale, r.gains[1], grad)
        r.gg[1] += jnp.sum((grad * fhat).reshape(TILE // 8, 8, width), axis=0)
        d_mid = drop_last(out_live + back).astype(BF16)
        r.mid[at, :] = d_mid
        r.wide[at, :] = widen(d_mid.astype(F32)).astype(BF16)
        fhat_one, _ = norm_parts(padded(r.xs[at, :]))
        r.nt[:, at] = (fhat_one * r.gains[0]).astype(BF16).T
        return carry

    for tile in range(tiles):
        mlp_end(tile, 0)
    out_store = pltpu.make_async_copy(r.ogs, out_hbm, r.out_sem.at[2])
    out_store.start()
    for piece in START + FIRST + DOWN:
        gather.drain(piece)
    gain_copy.wait_send()

    def back_step(p, carry):
        def project(tile, inner):
            at = wide_at(tile)
            wo = jnp.concatenate(
                [r.wbuf[0, 3, lane_at(HALF * y + LANE * p), :] for y in range(2)], 0
            )
            out = dot_rows(r.wide[at, :], wo).astype(BF16)
            r.do[0, at, :] = out[:, :LANE]
            r.do[1, at, :] = out[:, LANE:]
            return inner

        lax.fori_loop(0, tiles // 2, project, 0)

        def pair(y, inner):
            block = 2 * p + y
            first_head = 6 * y + 2 * p
            attn_rows = pl.ds(pl.multiple_of(HALF * y + LANE * p, LANE), LANE)
            product = r.do[y].T.astype(F32) * r.attnt[attn_rows, :].astype(F32)
            dots = [
                jnp.sum(product[i * HEAD_DIM : (i + 1) * HEAD_DIM, :], axis=0, keepdims=True)
                for i in range(2)
            ]
            lses = [r.lse[pl.ds(first_head + i, 1), :] for i in range(2)]
            r.dqt[...] = jnp.zeros_like(r.dqt)
            for kb in range(tiles):
                lo = kb * TILE
                at = pl.ds(lo, TILE)
                rest = pl.ds(lo, rows - lo)
                lane = lane_of((TILE, LANE))
                query = r.qkv[block, 0, rest, :] * BF16(HEAD_DIM**-0.5)
                keys = r.qkv[block, 1, at, :]
                values = r.qkv[block, 2, at, :]
                d_out = r.do[y, rest, :]
                bias = r.bias[at, rest].astype(F32)
                d_keys, d_values = [], []
                for i in range(2):
                    mine = (lane < HEAD_DIM) if i == 0 else (lane >= HEAD_DIM)
                    keys_mine = jnp.where(mine, keys, BF16(0))
                    scores = dot_rows(keys_mine, query) + bias
                    probs = jnp.exp(scores - lses[i][:, lo:])
                    d_probs = dot_rows(jnp.where(mine, values, BF16(0)), d_out)
                    d_scores = (probs * (d_probs - dots[i][:, lo:])).astype(BF16)
                    d_values.append(dot(probs.astype(BF16), d_out))
                    d_keys.append(dot(d_scores, query))
                    r.dqt[:, rest] += dot(keys_mine.T, d_scores)
                for t, parts in ((1, d_keys), (2, d_values)):
                    whole = jnp.where(lane < HEAD_DIM, parts[0], parts[1]).astype(BF16)
                    r.w2[p, pl.ds(2 * kb, 2), :, lane_at((3 * y + t) * LANE)] = whole.reshape(2, LANE, LANE)
            d_query = (r.dqt[...] * HEAD_DIM**-0.5).T.astype(BF16)
            r.w2[p, :, :, lane_at(3 * y * LANE)] = d_query.reshape(8, LANE, LANE)
            return inner

        lax.fori_loop(0, 2, pair, 0)

        def grads(half):
            own = half_rows(half)
            for n in range(4):
                if n < 3:
                    d_qkv = jnp.concatenate(
                        [
                            r.w2[p, :, :, pl.ds((3 * y + n) * LANE, LANE)].reshape(rows, LANE)
                            for y in range(2)
                        ],
                        1,
                    )
                    out = dot(r.nt[own, :], d_qkv).astype(BF16)
                else:
                    wide = jnp.concatenate(
                        [r.wide[:, lane_at(HALF * y + LANE * p)] for y in range(2)], 1
                    )
                    out = dot(r.attnt[own, :], wide).astype(BF16)
                for y in range(2):
                    r.gbig[4 * y + n, own, :] = out[:, y * LANE : (y + 1) * LANE]

        def half_step(step, inner):
            if not reduce:
                grads(step)
                return inner
            grads((1 - place.core) * (1 - step) + place.core * step)


            @pl.when(step == 0)
            def _():
                big.start(p + 3)

            return inner

        lax.fori_loop(0, 2, half_step, 0)
        if reduce:
            big.after_x(p, 1)
            big.after_z(p + 1, jnp.where(p == 2, 0, p + 1), jnp.where(p == 2, 0, 1))
            down.after_z(p)
            pl.when(p < 2)(lambda: down.after_y(p + 1))
            pl.when(p == 0)(lambda: down.after_x(2))
            big.after_y(p + 2)
            big.after_core(p + 3)
        if not reduce:
            dump(r.gbig, outs[0], p, 0)

        return carry

    lax.fori_loop(0, 3, back_step, 0)

    def back_end(tile, carry):
        at = tile_at(tile)
        fhat, scale = norm_parts(padded(r.xs[at, :]))
        d_qkv = jnp.concatenate(
            [r.w2[p, pl.ds(2 * tile, 2)].reshape(TILE, width) for p in range(3)], 1
        )
        w_in = jnp.concatenate([r.wbuf[0, p] for p in range(3)], 1)
        grad = dot_rows(d_qkv, w_in)
        back = norm_back(fhat, scale, r.gains[0], grad)
        r.gg[0] += jnp.sum((grad * fhat).reshape(TILE // 8, 8, width), axis=0)
        r.xs[at, :] = (r.mid[at, :].astype(F32) + back).astype(BF16)[:, : width - 1]
        return carry

    lax.fori_loop(0, tiles, back_end, 0)
    grad_store = pltpu.make_async_copy(r.xs, grad_hbm, r.out_sem.at[3])
    grad_store.start()

    gg = [jnp.sum(r.gg[i], axis=0, keepdims=True) for i in range(2)]
    row = lax.broadcasted_iota(jnp.int32, (8, width), 0)
    gain_rows = jnp.where(row == 0, gg[0], 0.0) + jnp.where(row == 1, gg[1], 0.0)
    if reduce:
        r.n_sum[...] = gain_rows

        def end_copy(chunk, half):
            block = r.g_acc.at[chunk, half_rows(half), :]
            return remote(block, block, r.end_sem.at[0, chunk], r.end_sem.at[1, chunk], place.core_id)

        norms.send(0)
        big.after_x(0, 0)
        end_copy(0, place.core).start()
        big.after_z(4, 1, 0)
        norms.receive(0)
        norms.send(1)
        big.after_y(5)
        norms.receive(1)
        norms.send(2)
        big.after_x(1, 0)
        end_copy(1, place.core).start()
        big.after_z(5, 2, 0)
        norms.receive(2)
        norms.send(3)
        big.after_x(2, 0)
        end_copy(2, place.core).start()
        norms.receive(3)
        for chunk in range(3):
            end_copy(chunk, place.core).wait_send()
            end_copy(chunk, 1 - place.core).wait_recv()
        stores = [
            pltpu.make_async_copy(r.g_acc, outs[0], r.out_sem.at[0]),
            pltpu.make_async_copy(r.d_acc, outs[1], r.out_sem.at[1]),
            pltpu.make_async_copy(r.n_sum, outs[2], r.out_sem.at[4]),
        ]
        for store in stores:
            store.start()
        for store in stores:
            store.wait()
    out_store.wait()
    grad_store.wait()
    return gain_rows


def plain_kernel(names, *args):
    gain_out, rest = args[9], args[:9] + args[10:]
    gain_out[...] = layer_kernel(False, names, *rest)


def sum_kernel(names, *args):
    layer_kernel(True, names, *args)


def finish_kernel(out_hbm, grad_hbm, acc_hbm, down_hbm, gain_hbm, *rest):
    out_to, grad_to, gain_to, first_to, down_to = rest[:5]
    streams, acc, down, gain, first_out, down_out, sems = rest[5:]
    dp, section = lax.axis_index("dp"), lax.axis_index("section")
    core = dp % 2
    loads = [
        pltpu.make_async_copy(out_hbm, streams.at[0], sems.at[0]),
        pltpu.make_async_copy(grad_hbm, streams.at[1], sems.at[1]),
        pltpu.make_async_copy(acc_hbm, acc, sems.at[2]),
        pltpu.make_async_copy(down_hbm, down, sems.at[3]),
        pltpu.make_async_copy(gain_hbm, gain, sems.at[4]),
    ]
    for load in loads:
        load.start()
    stores = []

    def store(source, target, index):
        stores.append(pltpu.make_async_copy(source, target, sems.at[index]))
        stores[-1].start()

    for k, target in ((0, out_to), (1, grad_to)):
        loads[k].wait()
        store(streams.at[k], target, k)
    loads[2].wait()
    half = LANE // 2

    @pl.when(core == 0)
    def _():
        first_out[:LANE, :] = acc[0].T
        first_out[LANE:, :] = acc[1].T[:half, :]

    @pl.when(core == 1)
    def _():
        first_out[:half, :] = acc[1].T[half:, :]
        first_out[half:, :] = acc[2].T

    store(first_out, first_to, 2)
    loads[3].wait()
    for p in range(3):
        for k in range(4):
            lo = (k // 2) * 6 * LANE + (k % 2) * 3 * LANE + p * LANE
            down_out[:, pl.ds(lo, LANE)] = down[p, k]
    store(down_out, down_to, 3)
    loads[4].wait()
    width = gain.shape[1]
    share = gain_to.shape[1]
    row = lax.broadcasted_iota(jnp.int32, gain.shape, 0)
    mine = jnp.sum(jnp.where(row == section, gain[...], 0.0), axis=0, keepdims=True)
    turned = pltpu.roll(jnp.broadcast_to(mine, gain.shape), (width - dp * share) % width, 1)
    gain_to[...] = turned[:1, :share]
    for copy in stores:
        copy.wait()


def per_device(stream_in, seq_len, live_rows, norm_gain, first_weight, down_weight, out_grad):
    rows, width = stream_in.shape[0], norm_gain.shape[1]
    reduce = lax.axis_size("dp") == 16
    shapes = scratch_of(rows, width, reduce)
    names = tuple(shapes)
    anywhere = pl.BlockSpec(memory_space=pl.ANY)
    in_vmem = pl.BlockSpec(memory_space=pltpu.VMEM)
    stream = jax.ShapeDtypeStruct((rows, width - 1), BF16)
    gains = jax.ShapeDtypeStruct((8, width), F32)
    if reduce:
        outs = [
            jax.ShapeDtypeStruct((3, width, LANE), F32),
            jax.ShapeDtypeStruct((3, 4, GROUP, LANE), F32),
            gains,
        ]
        out_specs = [anywhere] * 3
        kernel = functools.partial(sum_kernel, names)
    else:
        chunks = jax.ShapeDtypeStruct((3, 8, width, LANE), BF16)
        outs = [gains, chunks, chunks, chunks]
        out_specs = [in_vmem] + [anywhere] * 3
        kernel = functools.partial(plain_kernel, names)
    results = pl.pallas_call(
        kernel,
        out_shape=[stream, stream] + outs,
        in_specs=[
            pl.BlockSpec(memory_space=pltpu.SMEM), pl.BlockSpec(memory_space=pltpu.SMEM)
        ]
        + [anywhere] * 5,
        out_specs=[anywhere, anywhere] + out_specs,
        scratch_shapes=list(shapes.values()),
        compiler_params=pltpu.CompilerParams(
            vmem_limit_bytes=VMEM_LIMIT, collective_id=0, has_side_effects=True
        ),
        name="layer",
    )(seq_len, live_rows, stream_in, out_grad, norm_gain, first_weight[0], down_weight)
    if reduce:
        share = width // 16
        out, grad, gain_out, first_out, down_out = pl.pallas_call(
                finish_kernel,
                out_shape=[
                    stream,
                    stream,
                    jax.ShapeDtypeStruct((1, share), F32),
                    jax.ShapeDtypeStruct((3 * LANE // 2, width), F32),
                    jax.ShapeDtypeStruct((GROUP, 12 * LANE), F32),
                ],
                in_specs=[anywhere] * 5,
                out_specs=[anywhere, anywhere, in_vmem, anywhere, anywhere],
                scratch_shapes=[
                    pltpu.VMEM((2, rows, width - 1), BF16),
                    pltpu.VMEM((3, width, LANE), F32),
                    pltpu.VMEM((3, 4, GROUP, LANE), F32),
                    pltpu.VMEM((8, width), F32),
                    pltpu.VMEM((3 * LANE // 2, width), F32),
                    pltpu.VMEM((GROUP, 12 * LANE), F32),
                    pltpu.SemaphoreType.DMA((5,)),
                ],
                name="finish",
            )(*results)
        return (out, grad, gain_out, first_out.T[None], down_out.T)
    stream_out, stream_grad, gain, zero, one, two = results

    def columns(chunks, order):
        split = chunks.reshape((3,) + ((2, 4) if order else (4, 2)) + (width, LANE))
        turned = split.transpose((3, 2, 1, 0, 4) if order else (3, 1, 2, 0, 4))
        return turned.reshape(width, 3 * 8 * LANE)

    first_sum = jnp.stack([columns(zero, True), columns(one, True)])
    first_out = lax.psum_scatter(first_sum, "section", scatter_dimension=0, tiled=True)
    first_out = lax.psum_scatter(first_out, "dp", scatter_dimension=2, tiled=True)
    down_sum = columns(two, False).T
    down_out = lax.psum_scatter(down_sum, "section", scatter_dimension=0, tiled=True)
    down_out = lax.psum_scatter(down_out, "dp", scatter_dimension=1, tiled=True)
    gain_out = lax.psum_scatter(gain[:2], "section", scatter_dimension=0, tiled=True)
    gain_out = lax.psum_scatter(gain_out, "dp", scatter_dimension=1, tiled=True)
    return (stream_out, stream_grad, gain_out, first_out.astype(F32), down_out.astype(F32))


def solution(mesh):
    in_specs = (
        P(("dp", "section"), None),
        P("dp"),
        P("dp"),
        P("section", None),
        P("section", None, None),
        P("section", None),
        P(("dp", "section"), None),
    )
    out_specs = (
        P(("dp", "section"), None),
        P(("dp", "section"), None),
        P("section", "dp"),
        P("section", None, "dp"),
        P("section", "dp"),
    )
    return jax.shard_map(
        per_device, mesh=mesh, in_specs=in_specs, out_specs=out_specs, check_vma=False
    )
```

```python
import functools

import jax
import jax.numpy as jnp
from jax import lax
from jax.experimental import pallas as pl
from jax.experimental.pallas import tpu as pltpu
from jax.sharding import PartitionSpec as P

HEADS = 12
HEAD_DIM = 64
EPSILON = 1e-05
MASKED_SCORE = -1e30
LANE = 128
TILE = 256
F32 = jnp.float32
BF16 = jnp.bfloat16
VMEM_LIMIT = 66000000


def dot(left, right):
    return lax.dot_general(left, right, (((1,), (0,)), ((), ())), preferred_element_type=F32)


def dot_rows(left, right):
    return lax.dot_general(left, right, (((1,), (1,)), ((), ())), preferred_element_type=F32)


def dot_cols(left, right):
    return lax.dot_general(left, right, (((0,), (0,)), ((), ())), preferred_element_type=F32)


def lane_of(shape):
    return lax.broadcasted_iota(jnp.int32, shape, 1)


def padded(block):
    return jnp.pad(block.astype(F32), ((0, 0), (0, 1)))


def full_width(block):
    lane = lane_of(block.shape)
    last = block.shape[1] - 1
    kept = jnp.where(lane == last, 0.0, block)
    return jnp.where(lane == last, -jnp.sum(kept, axis=-1, keepdims=True), kept)


def norm_parts(block):
    full = full_width(block)
    scale = lax.rsqrt(jnp.mean(full * full, axis=-1, keepdims=True) + EPSILON)
    return full * scale, scale


def norm_back(fhat, scale, gain, grad):
    weighted = grad * gain
    inner = jnp.mean(weighted * fhat, axis=-1, keepdims=True)
    error = scale * (weighted - fhat * inner)
    last = error.shape[1] - 1
    tail = jnp.sum(jnp.where(lane_of(error.shape) == last, error, 0.0), axis=-1, keepdims=True)
    return error - tail


def drop_last(block):
    return jnp.where(lane_of(block.shape) == block.shape[1] - 1, 0.0, block)


def widen(block):
    return block - jnp.sum(block, axis=-1, keepdims=True) * (1.0 / block.shape[1])


def allowed_of(query_pos, key_pos, length, live_count):
    start = query_pos & (-length)
    usable = (key_pos < live_count) | (key_pos == query_pos)
    return (key_pos >= start) & (key_pos <= query_pos) & usable


MESH = pl.DeviceIdType.MESH
HALF = 384
PART = 192
GROUP = 48


class Refs:
    def __init__(self, **refs):
        self.__dict__.update(refs)


def scratch_of(rows, width, reduce):
    vmem = pltpu.VMEM
    dma = pltpu.SemaphoreType.DMA
    credit = pltpu.SemaphoreType.REGULAR
    shapes = dict(
        xs=vmem((rows, width - 1), BF16),
        ogs=vmem((rows, width - 1), BF16),
        wbuf=vmem((2, 4, width, width), BF16),
        w2=vmem((3, 8, LANE, width), BF16),
        gains=vmem((2, 1, width), F32),
        qkv=vmem((6, 3, rows, LANE), BF16),
        attnt=vmem((width, rows), BF16),
        mid=vmem((rows, width), BF16),
        nrm=vmem((rows, width), BF16),
        wide=vmem((rows, width), BF16),
        nt=vmem((width, rows), BF16),
        wt=vmem((width, rows), BF16),
        act=vmem((rows, 8 * LANE), BF16),
        dpre=vmem((rows, 8 * LANE), BF16),
        br=vmem((rows, width), F32),
        dn=vmem((rows, width), F32),
        bias=vmem((rows, rows), BF16),
        vt=vmem((LANE, rows), BF16),
        lse=vmem((16, rows), F32),
        do=vmem((2, rows, LANE), BF16),
        dqt=vmem((LANE, rows), F32),
        gg=vmem((2, 8, width), F32),
        gbig=vmem((8, width, LANE), BF16),
        gdown=vmem((8, width, LANE), BF16),
        load_sem=dma((10,)),
        out_sem=dma((5,)),
        ga_send=dma((8, 9)),
        ga_recv=dma((8, 9)),
    )
    if reduce:
        shapes.update(
            g_rc=vmem((8, HALF, LANE), BF16),
            g_keep=vmem((4, HALF, LANE), BF16),
            g_s1=vmem((4, HALF, LANE), BF16),
            g_r2=vmem((2, 4, HALF, LANE), BF16),
            g_s2=vmem((2, 3, HALF, LANE), BF16),
            g_own=vmem((2, HALF, LANE), BF16),
            g_rz=vmem((2, 3, HALF, LANE), BF16),
            g_sx=vmem((HALF, LANE), BF16),
            g_rx=vmem((3, HALF, LANE), BF16),
            g_acc=vmem((3, width, LANE), F32),
            d_rc=vmem((8, HALF, LANE), BF16),
            d_keep=vmem((4, HALF, LANE), BF16),
            d_s1=vmem((4, HALF, LANE), BF16),
            d_r2=vmem((2, 4, HALF, LANE), BF16),
            d_keep2=vmem((4, PART, LANE), BF16),
            d_s2=vmem((4, PART, LANE), BF16),
            d_ry=vmem((2, 4, PART, LANE), BF16),
            d_s3=vmem((3, 4, GROUP, LANE), BF16),
            d_own=vmem((4, GROUP, LANE), BF16),
            d_rz=vmem((2, 3, 4, GROUP, LANE), BF16),
            d_acc=vmem((3, 4, GROUP, LANE), F32),
            n_sum=vmem((8, width), F32),
            n_send=vmem((4, 8, width), F32),
            n_recv=vmem((6, 8, width), F32),
            core_sem=dma((2, 2)),
            gy_send=dma((4,)),
            gy_recv=dma((2, 4)),
            gz_send=dma((2, 3)),
            gz_recv=dma((2, 3)),
            x_sem=dma((4,)),
            dx_sem=dma((3,)),
            dy_sem=dma((3,)),
            dz_send=dma((3,)),
            dz_recv=dma((2, 3)),
            n_sem=dma((2, 6)),
            end_sem=dma((2, 3)),
            credit=credit((6,)),
            z_credit=credit((2, 3)),
        )
    return shapes


class Place:
    def __init__(self):
        self.dp = lax.axis_index("dp")
        self.section = lax.axis_index("section")
        self.core = self.dp % 2
        self.y = (self.dp // 2) % 2
        self.z = self.dp // 4
        self.pair = (self.dp // 4) % 2
        self.pair_id = {"dp": self.dp + 4 - 8 * self.pair}
        self.core_id = {"dp": self.dp + 1 - 2 * self.core}
        self.y_id = {"dp": self.dp + 2 - 4 * self.y}
        self.x_id = {"section": 1 - self.section}

    def z_of(self, r):
        return (self.z + r) % 4

    def z_back(self, r):
        return (self.z + 4 - r) % 4

    def z_id(self, r):
        return {"dp": self.dp + 4 * (self.z_of(r) - self.z)}

    def z_back_id(self, r):
        return {"dp": self.dp + 4 * (self.z_back(r) - self.z)}


def remote(source, target, send_sem, recv_sem, device):
    return pltpu.make_async_remote_copy(
        src_ref=source, dst_ref=target, send_sem=send_sem, recv_sem=recv_sem,
        device_id=device, device_id_type=MESH,
    )


def landed(target, send_sem, recv_sem, device):
    remote(target, target, send_sem, recv_sem, device).wait_recv()


def sent(source, send_sem, recv_sem, device):
    remote(source, source, send_sem, recv_sem, device).wait_send()


class Gather:
    def __init__(self, refs, place):
        self.refs, self.place = refs, place
        self.mine, self.theirs = place.section, 1 - place.section

    def block(self, slot, piece, part):
        kind, k = piece
        if kind == "down":
            size = LANE // 2
            rows = pl.ds(pl.multiple_of(size * (part % 2), size), size)
            return self.refs.w2.at[k, 4 * slot + part // 2, rows, :], k + 5
        size = PART // 2
        rows = pl.ds(pl.multiple_of(size * part, size), size)
        if kind == "start":
            return self.refs.wbuf.at[slot, 0, rows, pl.ds(HALF * k, HALF)], k
        return self.refs.wbuf.at[slot, k, rows, :], k + 1

    def part(self, z, y, core):
        return 4 * z + 2 * y + core

    def copy(self, kind, piece, slot, part, device):
        ref, at = self.block(slot, piece, part)
        return remote(ref, ref, self.refs.ga_send.at[kind, at], self.refs.ga_recv.at[kind, at], device)

    def routes(self, piece, core):
        p = self.place
        own = self.part(p.pair, p.y, core)
        from_y = self.part(p.pair, 1 - p.y, core)
        from_z = self.part(1 - p.pair, p.y, core)
        far = self.part(1 - p.pair, 1 - p.y, core)
        return own, from_y, from_z, far

    def send_x(self, piece):
        own = self.routes(piece, self.place.core)[0]
        self.copy(0, piece, self.mine, own, self.place.x_id).start()

    def across(self, piece, part):
        p = self.place
        device = {"dp": p.dp + p.core * (2 - 4 * p.y) + (1 - p.core) * (4 - 8 * p.pair)}
        return self.copy(3, piece, self.theirs, part, device)

    def forward(self, piece):
        p = self.place
        own = self.routes(piece, p.core)[0]
        self.copy(0, piece, self.theirs, own, p.x_id).wait_recv()
        self.copy(1, piece, self.theirs, own, p.y_id).start()
        self.copy(2, piece, self.theirs, own, p.pair_id).start()
        self.copy(4, piece, self.theirs, own, p.core_id).start()

    def relay(self, piece):
        p = self.place
        _, from_y, from_z, _ = self.routes(piece, p.core)
        self.copy(1, piece, self.theirs, from_y, p.y_id).wait_recv()
        self.copy(5, piece, self.theirs, from_y, p.core_id).start()
        self.copy(2, piece, self.theirs, from_z, p.pair_id).wait_recv()
        self.copy(6, piece, self.theirs, from_z, p.core_id).start()
        self.across(piece, p.core * from_z + (1 - p.core) * from_y).start()

    def close(self, piece):
        p = self.place
        far = self.routes(piece, p.core)[3]
        self.across(piece, far).wait_recv()
        self.copy(7, piece, self.theirs, far, p.core_id).start()

    def use(self, piece):
        p = self.place
        for kind, part in enumerate(self.routes(piece, 1 - p.core)):
            self.copy(4 + kind, piece, self.theirs, part, p.core_id).wait_recv()

    def drain(self, piece):
        p = self.place
        own, from_y, from_z, far = self.routes(piece, p.core)
        self.copy(0, piece, self.mine, own, p.x_id).wait_send()
        self.copy(1, piece, self.theirs, own, p.y_id).wait_send()
        self.copy(2, piece, self.theirs, own, p.pair_id).wait_send()
        self.across(piece, p.core * from_z + (1 - p.core) * from_y).wait_send()
        for kind, part in enumerate((own, from_y, from_z, far)):
            self.copy(4 + kind, piece, self.theirs, part, p.core_id).wait_send()


START = [("start", k) for k in range(2)]
FIRST = [("first", k) for k in range(1, 4)]
DOWN = [("down", k) for k in range(3)]


def half_rows(half):
    return pl.ds(pl.multiple_of(HALF * half, HALF), HALF)


def when(condition, action):
    if isinstance(condition, bool):
        if condition:
            action()
    else:
        pl.when(condition)(action)


class BigSum:
    jobs = 6

    def __init__(self, refs, place):
        self.r, self.p = refs, place

    def core_copy(self):
        r, p = self.r, self.p
        return remote(
            r.gbig.at[:, half_rows(1 - p.core), :], r.g_rc, r.core_sem.at[0, 0], r.core_sem.at[1, 0], p.core_id
        )

    def start(self, j):
        when(j >= 1, lambda: pl.semaphore_wait(self.r.credit.at[0], 1))
        self.core_copy().start()

    def y_copy(self, j, block):
        r, p = self.r, self.p
        return remote(
            r.g_s1.at[block], r.g_r2.at[j % 2, block], r.gy_send.at[block], r.gy_recv.at[j % 2, block], p.y_id
        )

    def after_core(self, j):
        r, p = self.r, self.p
        self.core_copy().wait()
        own = half_rows(p.core)
        when(j >= 2, lambda: pl.semaphore_wait(r.credit.at[1], 1))
        for k in range(4):
            z = p.z_of((k + 1) % 4)
            at = 4 * (1 - p.y) + z
            r.g_s1[z] = r.gbig[at, own, :] + r.g_rc[at]
            self.y_copy(j, z).start()
        for z in range(4):
            at = 4 * p.y + z
            r.g_keep[z] = r.gbig[at, own, :] + r.g_rc[at]
        when(
            j <= self.jobs - 2,
            lambda: pl.semaphore_signal(r.credit.at[0], inc=1, device_id=p.core_id, device_id_type=MESH),
        )

    def z_copy(self, j, k):
        r, p = self.r, self.p
        return remote(
            r.g_s2.at[j % 2, k - 1], r.g_rz.at[j % 2, k - 1], r.gz_send.at[j % 2, k - 1], r.gz_recv.at[j % 2, k - 1], p.z_id(k)
        )

    def after_y(self, j):
        r, p = self.r, self.p
        slot = j % 2
        for k in range(1, 4):
            z = p.z_of(k)
            self.y_copy(j, z).wait_recv()
            r.g_s2[slot, k - 1] = r.g_keep[z] + r.g_r2[slot, z]
            when(j >= 2, lambda k=k: pl.semaphore_wait(r.z_credit.at[0, k - 1], 1))
            self.z_copy(j, k).start()
        self.y_copy(j, p.z).wait_recv()
        r.g_own[slot] = r.g_keep[p.z] + r.g_r2[slot, p.z]
        for k in range(4):
            self.y_copy(j, k).wait_send()
        when(
            j <= self.jobs - 3,
            lambda: pl.semaphore_signal(r.credit.at[1], inc=1, device_id=p.y_id, device_id_type=MESH),
        )

    def x_copy(self, chunk):
        r, p = self.r, self.p
        return remote(r.g_sx, r.g_rx.at[chunk], r.x_sem.at[3], r.x_sem.at[chunk], p.x_id)

    def after_z(self, j, chunk, target):
        r, p = self.r, self.p
        slot = j % 2
        for k in range(1, 4):
            self.z_copy(j, k).wait()
        total = r.g_own[slot].astype(F32)
        for k in range(3):
            total = total + r.g_rz[slot, k].astype(F32)

        @pl.when(p.section != target)
        def _():
            r.g_sx[...] = total.astype(BF16)
            self.x_copy(chunk).start()

        @pl.when(p.section == target)
        def _():
            r.g_acc[chunk, half_rows(p.core), :] = total

        for k in range(1, 4):
            when(
                j <= self.jobs - 3,
                lambda k=k: pl.semaphore_signal(
                    r.z_credit.at[0, k - 1], inc=1, device_id=p.z_back_id(k), device_id_type=MESH
                ),
            )

    def after_x(self, chunk, target):
        r, p = self.r, self.p

        @pl.when(p.section != target)
        def _():
            self.x_copy(chunk).wait_send()

        @pl.when(p.section == target)
        def _():
            self.x_copy(chunk).wait_recv()
            own = half_rows(p.core)
            r.g_acc[chunk, own, :] = r.g_acc[chunk, own, :] + r.g_rx[chunk].astype(F32)


class DownSum:
    jobs = 3

    def __init__(self, refs, place):
        self.r, self.p = refs, place

    def core_copy(self):
        r, p = self.r, self.p
        return remote(
            r.gdown.at[:, half_rows(1 - p.core), :], r.d_rc, r.core_sem.at[0, 1], r.core_sem.at[1, 1], p.core_id
        )

    def start(self, j):
        when(j >= 1, lambda: pl.semaphore_wait(self.r.credit.at[2], 1))
        self.core_copy().start()

    def x_copy(self, j):
        r, p = self.r, self.p
        return remote(r.d_s1, r.d_r2.at[j % 2], r.dx_sem.at[2], r.dx_sem.at[j % 2], p.x_id)

    def after_core(self, j):
        r, p = self.r, self.p
        self.core_copy().wait()
        own = half_rows(p.core)
        for k in range(4):
            at = 4 * (1 - p.section) + k
            r.d_s1[k] = r.gdown[at, own, :] + r.d_rc[at]
        when(j >= 2, lambda: pl.semaphore_wait(r.credit.at[3], 1))
        self.x_copy(j).start()
        for k in range(4):
            at = 4 * p.section + k
            r.d_keep[k] = r.gdown[at, own, :] + r.d_rc[at]
        when(
            j <= self.jobs - 2,
            lambda: pl.semaphore_signal(r.credit.at[2], inc=1, device_id=p.core_id, device_id_type=MESH),
        )

    def y_copy(self, j):
        r, p = self.r, self.p
        return remote(r.d_s2, r.d_ry.at[j % 2], r.dy_sem.at[2], r.dy_sem.at[j % 2], p.y_id)

    def after_x(self, j):
        r, p = self.r, self.p
        slot = j % 2
        self.x_copy(j).wait()
        theirs = pl.ds(pl.multiple_of(PART * (1 - p.y), PART), PART)
        mine = pl.ds(pl.multiple_of(PART * p.y, PART), PART)
        for k in range(4):
            r.d_s2[k] = r.d_keep[k, theirs, :] + r.d_r2[slot, k, theirs, :]
        when(j >= 2, lambda: pl.semaphore_wait(r.credit.at[4], 1))
        self.y_copy(j).start()
        for k in range(4):
            r.d_keep2[k] = r.d_keep[k, mine, :] + r.d_r2[slot, k, mine, :]
        when(
            j <= self.jobs - 3,
            lambda: pl.semaphore_signal(r.credit.at[3], inc=1, device_id=p.x_id, device_id_type=MESH),
        )

    def z_copy(self, j, k):
        r, p = self.r, self.p
        return remote(
            r.d_s3.at[k - 1], r.d_rz.at[j % 2, k - 1], r.dz_send.at[k - 1], r.dz_recv.at[j % 2, k - 1], p.z_id(k)
        )

    def after_y(self, j):
        r, p = self.r, self.p
        slot = j % 2
        self.y_copy(j).wait()
        for k in range(4):
            rows = pl.ds(pl.multiple_of(GROUP * p.z_of(k), GROUP), GROUP)
            for f in range(4):
                total = r.d_keep2[f, rows, :] + r.d_ry[slot, f, rows, :]
                if k == 0:
                    r.d_own[f] = total
                else:
                    r.d_s3[k - 1, f] = total
        for k in range(1, 4):
            when(j >= 2, lambda k=k: pl.semaphore_wait(r.z_credit.at[1, k - 1], 1))
            self.z_copy(j, k).start()
        when(
            j <= self.jobs - 3,
            lambda: pl.semaphore_signal(r.credit.at[4], inc=1, device_id=p.y_id, device_id_type=MESH),
        )

    def after_z(self, j):
        r, p = self.r, self.p
        slot = j % 2
        for k in range(1, 4):
            self.z_copy(j, k).wait()
        for f in range(4):
            total = r.d_own[f].astype(F32)
            for k in range(3):
                total = total + r.d_rz[slot, k, f].astype(F32)
            r.d_acc[j, f] = total
        for k in range(1, 4):
            when(
                j <= self.jobs - 3,
                lambda k=k: pl.semaphore_signal(
                    r.z_credit.at[1, k - 1], inc=1, device_id=p.z_back_id(k), device_id_type=MESH
                ),
            )


class NormSum:
    def __init__(self, refs, place):
        self.r, self.p = refs, place

    def copy(self, stage, slot, device):
        r = self.r
        return remote(
            r.n_send.at[stage], r.n_recv.at[slot], r.n_sem.at[0, slot], r.n_sem.at[1, slot], device
        )

    def routes(self, stage):
        p = self.p
        return [
            [(0, p.core_id)], [(1, p.y_id)], [(2, p.z_id(1)), (3, p.z_id(2)), (4, p.z_id(3))], [(5, p.x_id)]
        ][stage]

    def send(self, stage):
        r = self.r
        r.n_send[stage] = r.n_sum[...]
        for slot, device in self.routes(stage):
            self.copy(stage, slot, device).start()

    def receive(self, stage):
        r = self.r
        for slot, device in self.routes(stage):
            self.copy(stage, slot, device).wait()
            r.n_sum[...] += r.n_recv[slot]


def layer_kernel(reduce, names, length_ref, live_ref, x_hbm, og_hbm, gain_in, first_hbm, down_hbm, out_hbm, grad_hbm, *rest):
    outs = rest[:3]
    r = Refs(**dict(zip(names, rest[3:])))
    place = Place()
    rows, width = r.mid.shape
    tiles = rows // TILE
    section = place.section
    length, live_count = length_ref[0], live_ref[0] - section * rows
    gather = Gather(r, place)
    big, down, norms = BigSum(r, place), DownSum(r, place), NormSum(r, place)

    def tile_at(tile):
        return pl.ds(pl.multiple_of(tile * TILE, TILE), TILE)

    def wide_at(tile):
        return pl.ds(pl.multiple_of(tile * 2 * TILE, 2 * TILE), 2 * TILE)

    def lane_at(lo):
        return pl.ds(pl.multiple_of(lo, LANE), LANE)

    def load(source, target, index):
        return pltpu.make_async_copy(source, target, r.load_sem.at[index])

    barrier = pltpu.get_barrier_semaphore()
    greeted = [place.core_id, place.y_id, place.x_id]
    greeted += [place.z_id(k) for k in range(1, 4)] if reduce else [place.pair_id]
    for device in greeted:
        pl.semaphore_signal(barrier, inc=1, device_id=device, device_id_type=MESH)
    x_load = load(x_hbm, r.xs, 7)
    og_load = load(og_hbm, r.ogs, 8)
    gain_load = load(gain_in, r.gains.at[section], 9)
    gain_load.start()
    for k in range(3):
        for z in range(3):
            for y in range(2):
                lo = width * z + HALF * y + LANE * k
                load(
                    first_hbm.at[:, pl.ds(lo, LANE)],
                    r.wbuf.at[section, k, :, pl.ds((3 * y + z) * LANE, LANE)],
                    k,
                ).start()
        if k == 0:
            x_load.start()
    load(first_hbm.at[:, pl.ds(3 * width, width)], r.wbuf.at[section, 3], 3).start()
    og_load.start()
    for k in range(3):
        for z in range(2):
            for y in range(2):
                lo = width * z + HALF * y + LANE * k
                load(
                    down_hbm.at[pl.ds(lo, LANE), :], r.w2.at[k, 4 * section + 2 * z + y], 4 + k
                ).start()

    gain_load.wait()
    pl.semaphore_wait(barrier, len(greeted))

    gain_ref = r.gains.at[section]
    gain_copy = remote(gain_ref, gain_ref, r.ga_send.at[0, 8], r.ga_recv.at[0, 8], place.x_id)
    gain_copy.start()
    for k in range(4):
        load(r.wbuf.at[section, k], r.wbuf.at[section, k], k).wait()
        for piece in START if k == 0 else [("first", k)]:
            gather.send_x(piece)
    for k in range(3):
        mine = r.w2.at[k, pl.ds(4 * section, 4)]
        load(mine, mine, 4 + k).wait()
        gather.send_x(("down", k))
    og_load.wait()

    def live_of(tile):
        row = tile * TILE + lax.broadcasted_iota(jnp.int32, (TILE, 1), 0)
        return (row < live_count).astype(F32)

    for tile in range(tiles):
        at = tile_at(tile)
        out_live = padded(r.ogs[at, :]) * live_of(tile)
        wide = widen(out_live).astype(BF16)
        r.wide[at, :] = wide
        turned = wide.T
        if reduce:
            for z in range(4):
                for y in range(2):
                    for c in range(2):
                        lo = PART * z + 2 * GROUP * y + GROUP * c
                        to = HALF * c + PART * y + GROUP * z
                        r.wt[pl.ds(to, GROUP), at] = turned[lo : lo + GROUP, :]
        else:
            r.wt[:, at] = turned

    x_load.wait()
    theirs = r.gains.at[1 - section]
    landed(theirs, r.ga_send.at[0, 8], r.ga_recv.at[0, 8], place.x_id)

    def begin_step(tile, carry):
        at = tile_at(tile)
        fhat, _ = norm_parts(padded(r.xs[at, :]))
        r.nrm[at, :] = (fhat * r.gains[0]).astype(BF16)
        key = tile * TILE + lax.broadcasted_iota(jnp.int32, (TILE, rows), 0)
        query = lax.broadcasted_iota(jnp.int32, (TILE, rows), 1)
        allowed = allowed_of(query, key, length, live_count)
        r.bias[at, :] = jnp.where(allowed, 0.0, MASKED_SCORE).astype(BF16)
        return carry

    lax.fori_loop(0, tiles, begin_step, 0)
    gather.forward(START[0])
    gather.forward(START[1])
    gather.relay(START[0])
    gather.forward(FIRST[0])
    gather.relay(START[1])
    gather.close(START[0])

    def project_half(y):
        lanes = pl.ds(HALF * y, HALF)

        pl.when(section == 1)(lambda: gather.use(START[y]))

        def project(tile, inner):
            at = wide_at(tile)
            out = dot(r.nrm[at, :], r.wbuf[0, 0, :, lanes]).astype(BF16)
            for t in range(3):
                r.qkv[y, t, at, :] = out[:, t * LANE : (t + 1) * LANE]
            return inner

        lax.fori_loop(0, tiles // 2, project, 0)

    def attention_step(p, carry):
        def project(tile, inner):
            at = wide_at(tile)
            out = dot(r.nrm[at, :], r.wbuf[0, p]).astype(BF16)
            for t in range(3):
                for y in range(2):
                    lo = (3 * y + t) * LANE
                    r.qkv[2 * p + y, t, at, :] = out[:, lo : lo + LANE]
            return inner

        @pl.when(p >= 1)
        def _():
            lax.fori_loop(0, tiles // 2, project, 0)

        def pair(y, inner):
            block = 2 * p + y
            first_head = 6 * y + 2 * p

            turn = 2 * p + y

            def at_turn(number, *actions):
                @pl.when(turn == number)
                def _():
                    for action, argument in actions:
                        action(argument)

            first, second, third = FIRST
            at_turn(
                0,
                (project_half, 0),
                (gather.close, START[1]),
                (gather.relay, first),
                (gather.forward, second),
            )
            at_turn(1, (project_half, 1))
            at_turn(2, (gather.relay, second), (gather.forward, third))
            at_turn(4, (gather.relay, third))
            r.vt[...] = r.qkv[block, 2].T
            out_rows = pl.multiple_of(HALF * y + LANE * p, LANE)

            def scores_of(qb, i):
                count = (qb + 1) * TILE
                at = pl.ds(qb * TILE, TILE)
                lane = lane_of((TILE, LANE))
                mine = (lane < HEAD_DIM) if i == 0 else (lane >= HEAD_DIM)
                query = jnp.where(mine, r.qkv[block, 0, at, :] * BF16(HEAD_DIM**-0.5), BF16(0))
                keys = r.qkv[block, 1, pl.ds(0, count), :]
                return dot_rows(keys, query) + r.bias[pl.ds(0, count), at].astype(F32)

            def mix(qb, i, scores):
                count = (qb + 1) * TILE
                at = pl.ds(qb * TILE, TILE)
                top = jnp.max(scores, axis=0, keepdims=True)
                terms = jnp.exp(scores - top).astype(BF16)
                values = jnp.concatenate(
                    [r.vt[pl.ds(i * HEAD_DIM, HEAD_DIM), pl.ds(0, count)], jnp.ones((16, count), BF16)], 0
                )
                out = dot(values, terms)
                total = out[HEAD_DIM : HEAD_DIM + 1, :]
                r.lse[pl.ds(first_head + i, 1), at] = top + jnp.log(total)
                r.attnt[pl.ds(out_rows + i * HEAD_DIM, HEAD_DIM), at] = (
                    out[:HEAD_DIM, :] / total
                ).astype(BF16)

            waiting = None
            for qb in range(tiles):
                for i in range(2):
                    scores = scores_of(qb, i)
                    if waiting is not None:
                        mix(*waiting)
                    waiting = (qb, i, scores)
            mix(*waiting)
            at_turn(1, (gather.close, first))
            at_turn(3, (gather.close, second))
            at_turn(4, (gather.forward, DOWN[0]))
            at_turn(5, (gather.close, third), (gather.relay, DOWN[0]), (gather.forward, DOWN[1]))
            return inner

        lax.fori_loop(0, 2, pair, 0)
        pl.when(section == 1)(lambda: gather.use(("first", p + 1)))
        return carry

    lax.fori_loop(0, 3, attention_step, 0)

    def attention_end(tile, carry):
        at = tile_at(tile)
        branch = dot_cols(r.attnt[:, at], r.wbuf[0, 3])
        mean = jnp.sum(branch, axis=-1, keepdims=True) * (1.0 / width)
        mid = drop_last(padded(r.xs[at, :]) + branch - mean).astype(BF16)
        r.mid[at, :] = mid
        fhat, _ = norm_parts(mid.astype(F32))
        norm = (fhat * r.gains[1]).astype(BF16)
        r.nrm[at, :] = norm
        r.nt[:, at] = norm.T
        return carry

    for tile in range(tiles):
        attention_end(tile, 0)

    gather.close(DOWN[0])
    gather.forward(DOWN[2])
    gather.relay(DOWN[1])

    @pl.when(section == 0)
    def _():
        for piece in START + FIRST:
            gather.use(piece)

    r.br[...] = jnp.zeros_like(r.br)
    r.dn[...] = jnp.zeros_like(r.dn)

    def dump(source, output, chunk, index):
        copy = pltpu.make_async_copy(source, output.at[chunk], r.out_sem.at[index])
        copy.start()
        copy.wait()

    def mlp_step(p, carry):
        gather.use(("down", p))

        def first_columns(n):
            if n < 3:
                return jnp.concatenate(
                    [r.wbuf[1, p, :, pl.ds((3 * y + n) * LANE, LANE)] for y in range(2)], 1
                )
            return jnp.concatenate(
                [r.wbuf[1, 3, :, lane_at(HALF * y + LANE * p)] for y in range(2)], 1
            )

        def hidden(tile, n):
            at = tile_at(tile)
            col = pl.ds(n * TILE, TILE)
            pre = dot(r.nrm[at, :], first_columns(n))
            d_act = dot_rows(r.wide[at, :], r.w2[p, pl.ds(2 * n, 2)].reshape(TILE, width))
            square = pre * pre
            inner_arg = pre * (0.7978845608028654 + (0.044715 * 0.7978845608028654) * square)
            tanh = jnp.tanh(inner_arg)
            half = 0.5 + 0.5 * tanh
            slope = half + (0.5 * pre) * (1.0 - tanh * tanh) * (
                0.7978845608028654 + (3.0 * 0.044715 * 0.7978845608028654) * square
            )
            r.act[at, col] = (pre * half).astype(BF16)
            r.dpre[at, col] = (d_act * slope).astype(BF16)

        def branch_part(tile, m):
            at = tile_at(tile)
            col = pl.ds(m * TILE, TILE)
            w2 = r.w2[p, :, :, col].reshape(8 * LANE, TILE)
            r.br[at, col] += dot(r.act[at, :], w2)

        def norm_part(tile, m):
            at = tile_at(tile)
            col = pl.ds(m * TILE, TILE)
            w1 = jnp.concatenate(
                [
                    r.wbuf[1, p, col, pl.ds((3 * y + z) * LANE, LANE)]
                    for z in range(3)
                    for y in range(2)
                ]
                + [r.wbuf[1, 3, col, lane_at(HALF * y + LANE * p)] for y in range(2)],
                1,
            )
            r.dn[at, col] += dot_rows(r.dpre[at, :], w1)

        for n in range(4):
            hidden(0, n)

        def rows_step(tile, inner):
            for n in range(4):
                hidden(tile, n)
                if n < 3:
                    branch_part(tile - 1, n)
                    norm_part(tile - 1, n)
            return inner

        lax.fori_loop(1, tiles, rows_step, 0)
        for n in range(3):
            branch_part(tiles - 1, n)
            norm_part(tiles - 1, n)

        @pl.when(p == 0)
        def _():
            gather.close(DOWN[1])
            gather.relay(DOWN[2])

        def grads(half):
            own = half_rows(half)
            for n in range(4):
                g1 = dot(r.nt[own, :], r.dpre[:, pl.ds(n * TILE, TILE)]).astype(BF16)
                for y in range(2):
                    r.gbig[4 * y + n, own, :] = g1[:, y * LANE : (y + 1) * LANE]

        def down_grads(half):
            own = half_rows(half)
            for n in range(4):
                g2 = dot(r.wt[own, :], r.act[:, pl.ds(n * TILE, TILE)]).astype(BF16)
                for y in range(2):
                    r.gdown[2 * n + y, own, :] = g2[:, y * LANE : (y + 1) * LANE]

        def half_step(step, inner):
            if not reduce:
                grads(step)
                down_grads(step)
                return inner
            half = (1 - place.core) * (1 - step) + place.core * step
            grads(half)
            pl.when(step == 0)(lambda: big.start(p))
            down_grads(half)
            pl.when(step == 0)(lambda: down.start(p))
            return inner

        lax.fori_loop(0, 2, half_step, 0)
        if reduce:

            @pl.when(p == 2)
            def _():
                big.after_z(0, 0, 1)
                down.after_y(0)

            @pl.when(p >= 1)
            def _():
                big.after_y(p - 1)
                down.after_x(p - 1)

            big.after_core(p)
            down.after_core(p)
            pl.when(p == 0)(lambda: gather.close(DOWN[2]))
        if not reduce:
            pl.when(p == 0)(lambda: gather.close(DOWN[2]))
            dump(r.gbig, outs[1], p, 0)
            dump(r.gdown, outs[2], p, 1)
        return carry

    lax.fori_loop(0, 3, mlp_step, 0)
    r.gg[...] = jnp.zeros_like(r.gg)

    def mlp_end(tile, carry):
        at = tile_at(tile)
        live = live_of(tile)
        mid = r.mid[at, :].astype(F32)
        out_live = padded(r.ogs[at, :]) * live
        branch = r.br[at, :]
        mean = jnp.sum(branch, axis=-1, keepdims=True) * (1.0 / width)
        out = ((mid + branch - mean) * live).astype(BF16)
        r.ogs[at, :] = out[:, : width - 1]
        fhat, scale = norm_parts(mid)
        grad = r.dn[at, :]
        back = norm_back(fhat, scale, r.gains[1], grad)
        r.gg[1] += jnp.sum((grad * fhat).reshape(TILE // 8, 8, width), axis=0)
        d_mid = drop_last(out_live + back).astype(BF16)
        r.mid[at, :] = d_mid
        r.wide[at, :] = widen(d_mid.astype(F32)).astype(BF16)
        fhat_one, _ = norm_parts(padded(r.xs[at, :]))
        r.nt[:, at] = (fhat_one * r.gains[0]).astype(BF16).T
        return carry

    for tile in range(tiles):
        mlp_end(tile, 0)
    out_store = pltpu.make_async_copy(r.ogs, out_hbm, r.out_sem.at[2])
    out_store.start()
    for piece in START + FIRST + DOWN:
        gather.drain(piece)
    gain_copy.wait_send()

    def back_step(p, carry):
        def project(tile, inner):
            at = wide_at(tile)
            wo = jnp.concatenate(
                [r.wbuf[0, 3, lane_at(HALF * y + LANE * p), :] for y in range(2)], 0
            )
            out = dot_rows(r.wide[at, :], wo).astype(BF16)
            r.do[0, at, :] = out[:, :LANE]
            r.do[1, at, :] = out[:, LANE:]
            return inner

        lax.fori_loop(0, tiles // 2, project, 0)

        def pair(y, inner):
            block = 2 * p + y
            first_head = 6 * y + 2 * p
            attn_rows = pl.ds(pl.multiple_of(HALF * y + LANE * p, LANE), LANE)
            product = r.do[y].T.astype(F32) * r.attnt[attn_rows, :].astype(F32)
            dots = [
                jnp.sum(product[i * HEAD_DIM : (i + 1) * HEAD_DIM, :], axis=0, keepdims=True)
                for i in range(2)
            ]
            lses = [r.lse[pl.ds(first_head + i, 1), :] for i in range(2)]
            r.dqt[...] = jnp.zeros_like(r.dqt)
            for kb in range(tiles):
                lo = kb * TILE
                at = pl.ds(lo, TILE)
                rest = pl.ds(lo, rows - lo)
                lane = lane_of((TILE, LANE))
                query = r.qkv[block, 0, rest, :] * BF16(HEAD_DIM**-0.5)
                keys = r.qkv[block, 1, at, :]
                values = r.qkv[block, 2, at, :]
                d_out = r.do[y, rest, :]
                bias = r.bias[at, rest].astype(F32)
                d_keys, d_values = [], []
                for i in range(2):
                    mine = (lane < HEAD_DIM) if i == 0 else (lane >= HEAD_DIM)
                    keys_mine = jnp.where(mine, keys, BF16(0))
                    scores = dot_rows(keys_mine, query) + bias
                    probs = jnp.exp(scores - lses[i][:, lo:])
                    d_probs = dot_rows(jnp.where(mine, values, BF16(0)), d_out)
                    d_scores = (probs * (d_probs - dots[i][:, lo:])).astype(BF16)
                    d_values.append(dot(probs.astype(BF16), d_out))
                    d_keys.append(dot(d_scores, query))
                    r.dqt[:, rest] += dot(keys_mine.T, d_scores)
                for t, parts in ((1, d_keys), (2, d_values)):
                    whole = jnp.where(lane < HEAD_DIM, parts[0], parts[1]).astype(BF16)
                    r.w2[p, pl.ds(2 * kb, 2), :, lane_at((3 * y + t) * LANE)] = whole.reshape(2, LANE, LANE)
            d_query = (r.dqt[...] * HEAD_DIM**-0.5).T.astype(BF16)
            r.w2[p, :, :, lane_at(3 * y * LANE)] = d_query.reshape(8, LANE, LANE)
            if reduce:

                @pl.when(jnp.logical_and(p == 0, y == 1))
                def _():
                    down.after_z(0)
                    down.after_y(1)
                    down.after_x(2)

                @pl.when(jnp.logical_and(p == 1, y == 0))
                def _():
                    down.after_z(1)
                    down.after_y(2)

                @pl.when(jnp.logical_and(p == 2, y == 1))
                def _():
                    down.after_z(2)

            return inner

        lax.fori_loop(0, 2, pair, 0)

        def grads(half):
            own = half_rows(half)
            for n in range(4):
                if n < 3:
                    d_qkv = jnp.concatenate(
                        [
                            r.w2[p, :, :, pl.ds((3 * y + n) * LANE, LANE)].reshape(rows, LANE)
                            for y in range(2)
                        ],
                        1,
                    )
                    out = dot(r.nt[own, :], d_qkv).astype(BF16)
                else:
                    wide = jnp.concatenate(
                        [r.wide[:, lane_at(HALF * y + LANE * p)] for y in range(2)], 1
                    )
                    out = dot(r.attnt[own, :], wide).astype(BF16)
                for y in range(2):
                    r.gbig[4 * y + n, own, :] = out[:, y * LANE : (y + 1) * LANE]

        def half_step(step, inner):
            if not reduce:
                grads(step)
                return inner
            grads((1 - place.core) * (1 - step) + place.core * step)


            @pl.when(step == 0)
            def _():
                big.start(p + 3)
                big.after_x(p, 1)
                big.after_z(p + 1, jnp.where(p == 2, 0, p + 1), jnp.where(p == 2, 0, 1))
                big.after_y(p + 2)

            return inner

        lax.fori_loop(0, 2, half_step, 0)
        if reduce:
            big.after_core(p + 3)
        if not reduce:
            dump(r.gbig, outs[0], p, 0)

        return carry

    lax.fori_loop(0, 3, back_step, 0)

    def back_end(tile, carry):
        at = tile_at(tile)
        fhat, scale = norm_parts(padded(r.xs[at, :]))
        d_qkv = jnp.concatenate(
            [r.w2[p, pl.ds(2 * tile, 2)].reshape(TILE, width) for p in range(3)], 1
        )
        w_in = jnp.concatenate([r.wbuf[0, p] for p in range(3)], 1)
        grad = dot_rows(d_qkv, w_in)
        back = norm_back(fhat, scale, r.gains[0], grad)
        r.gg[0] += jnp.sum((grad * fhat).reshape(TILE // 8, 8, width), axis=0)
        r.xs[at, :] = (r.mid[at, :].astype(F32) + back).astype(BF16)[:, : width - 1]
        return carry

    lax.fori_loop(0, tiles, back_end, 0)
    grad_store = pltpu.make_async_copy(r.xs, grad_hbm, r.out_sem.at[3])
    grad_store.start()

    gg = [jnp.sum(r.gg[i], axis=0, keepdims=True) for i in range(2)]
    row = lax.broadcasted_iota(jnp.int32, (8, width), 0)
    gain_rows = jnp.where(row == 0, gg[0], 0.0) + jnp.where(row == 1, gg[1], 0.0)
    if reduce:
        r.n_sum[...] = gain_rows

        def end_copy(chunk, half):
            block = r.g_acc.at[chunk, half_rows(half), :]
            return remote(block, block, r.end_sem.at[0, chunk], r.end_sem.at[1, chunk], place.core_id)

        norms.send(0)
        big.after_x(0, 0)
        end_copy(0, place.core).start()
        big.after_y(5)
        norms.receive(0)
        norms.send(1)
        big.after_z(4, 1, 0)
        norms.receive(1)
        norms.send(2)
        big.after_x(1, 0)
        end_copy(1, place.core).start()
        big.after_z(5, 2, 0)
        norms.receive(2)
        norms.send(3)
        big.after_x(2, 0)
        end_copy(2, place.core).start()
        norms.receive(3)
        for chunk in range(3):
            end_copy(chunk, place.core).wait_send()
            end_copy(chunk, 1 - place.core).wait_recv()
        stores = [
            pltpu.make_async_copy(r.g_acc, outs[0], r.out_sem.at[0]),
            pltpu.make_async_copy(r.d_acc, outs[1], r.out_sem.at[1]),
            pltpu.make_async_copy(r.n_sum, outs[2], r.out_sem.at[4]),
        ]
        for store in stores:
            store.start()
        for store in stores:
            store.wait()
    out_store.wait()
    grad_store.wait()
    return gain_rows


def plain_kernel(names, *args):
    gain_out, rest = args[9], args[:9] + args[10:]
    gain_out[...] = layer_kernel(False, names, *rest)


def sum_kernel(names, *args):
    layer_kernel(True, names, *args)


def finish_kernel(out_hbm, grad_hbm, acc_hbm, down_hbm, gain_hbm, *rest):
    out_to, grad_to, gain_to, first_to, down_to = rest[:5]
    streams, acc, down, gain, first_out, down_out, sems = rest[5:]
    dp, section = lax.axis_index("dp"), lax.axis_index("section")
    core = dp % 2
    loads = [
        pltpu.make_async_copy(out_hbm, streams.at[0], sems.at[0]),
        pltpu.make_async_copy(grad_hbm, streams.at[1], sems.at[1]),
        pltpu.make_async_copy(acc_hbm, acc, sems.at[2]),
        pltpu.make_async_copy(down_hbm, down, sems.at[3]),
        pltpu.make_async_copy(gain_hbm, gain, sems.at[4]),
    ]
    for load in loads:
        load.start()
    stores = []

    def store(source, target, index):
        stores.append(pltpu.make_async_copy(source, target, sems.at[index]))
        stores[-1].start()

    for k, target in ((0, out_to), (1, grad_to)):
        loads[k].wait()
        store(streams.at[k], target, k)
    loads[2].wait()
    half = LANE // 2

    @pl.when(core == 0)
    def _():
        first_out[:LANE, :] = acc[0].T
        first_out[LANE:, :] = acc[1].T[:half, :]

    @pl.when(core == 1)
    def _():
        first_out[:half, :] = acc[1].T[half:, :]
        first_out[half:, :] = acc[2].T

    store(first_out, first_to, 2)
    loads[3].wait()
    for p in range(3):
        for k in range(4):
            lo = (k // 2) * 6 * LANE + (k % 2) * 3 * LANE + p * LANE
            down_out[:, pl.ds(lo, LANE)] = down[p, k]
    store(down_out, down_to, 3)
    loads[4].wait()
    width = gain.shape[1]
    share = gain_to.shape[1]
    row = lax.broadcasted_iota(jnp.int32, gain.shape, 0)
    mine = jnp.sum(jnp.where(row == section, gain[...], 0.0), axis=0, keepdims=True)
    turned = pltpu.roll(jnp.broadcast_to(mine, gain.shape), (width - dp * share) % width, 1)
    gain_to[...] = turned[:1, :share]
    for copy in stores:
        copy.wait()


def per_device(stream_in, seq_len, live_rows, norm_gain, first_weight, down_weight, out_grad):
    rows, width = stream_in.shape[0], norm_gain.shape[1]
    reduce = lax.axis_size("dp") == 16
    shapes = scratch_of(rows, width, reduce)
    names = tuple(shapes)
    anywhere = pl.BlockSpec(memory_space=pl.ANY)
    in_vmem = pl.BlockSpec(memory_space=pltpu.VMEM)
    stream = jax.ShapeDtypeStruct((rows, width - 1), BF16)
    gains = jax.ShapeDtypeStruct((8, width), F32)
    if reduce:
        outs = [
            jax.ShapeDtypeStruct((3, width, LANE), F32),
            jax.ShapeDtypeStruct((3, 4, GROUP, LANE), F32),
            gains,
        ]
        out_specs = [anywhere] * 3
        kernel = functools.partial(sum_kernel, names)
    else:
        chunks = jax.ShapeDtypeStruct((3, 8, width, LANE), BF16)
        outs = [gains, chunks, chunks, chunks]
        out_specs = [in_vmem] + [anywhere] * 3
        kernel = functools.partial(plain_kernel, names)
    results = pl.pallas_call(
        kernel,
        out_shape=[stream, stream] + outs,
        in_specs=[
            pl.BlockSpec(memory_space=pltpu.SMEM), pl.BlockSpec(memory_space=pltpu.SMEM)
        ]
        + [anywhere] * 5,
        out_specs=[anywhere, anywhere] + out_specs,
        scratch_shapes=list(shapes.values()),
        compiler_params=pltpu.CompilerParams(
            vmem_limit_bytes=VMEM_LIMIT, collective_id=0, has_side_effects=True
        ),
        name="layer",
    )(seq_len, live_rows, stream_in, out_grad, norm_gain, first_weight[0], down_weight)
    if reduce:
        share = width // 16
        out, grad, gain_out, first_out, down_out = pl.pallas_call(
                finish_kernel,
                out_shape=[
                    stream,
                    stream,
                    jax.ShapeDtypeStruct((1, share), F32),
                    jax.ShapeDtypeStruct((3 * LANE // 2, width), F32),
                    jax.ShapeDtypeStruct((GROUP, 12 * LANE), F32),
                ],
                in_specs=[anywhere] * 5,
                out_specs=[anywhere, anywhere, in_vmem, anywhere, anywhere],
                scratch_shapes=[
                    pltpu.VMEM((2, rows, width - 1), BF16),
                    pltpu.VMEM((3, width, LANE), F32),
                    pltpu.VMEM((3, 4, GROUP, LANE), F32),
                    pltpu.VMEM((8, width), F32),
                    pltpu.VMEM((3 * LANE // 2, width), F32),
                    pltpu.VMEM((GROUP, 12 * LANE), F32),
                    pltpu.SemaphoreType.DMA((5,)),
                ],
                name="finish",
            )(*results)
        return (out, grad, gain_out, first_out.T[None], down_out.T)
    stream_out, stream_grad, gain, zero, one, two = results

    def columns(chunks, order):
        split = chunks.reshape((3,) + ((2, 4) if order else (4, 2)) + (width, LANE))
        turned = split.transpose((3, 2, 1, 0, 4) if order else (3, 1, 2, 0, 4))
        return turned.reshape(width, 3 * 8 * LANE)

    first_sum = jnp.stack([columns(zero, True), columns(one, True)])
    first_out = lax.psum_scatter(first_sum, "section", scatter_dimension=0, tiled=True)
    first_out = lax.psum_scatter(first_out, "dp", scatter_dimension=2, tiled=True)
    down_sum = columns(two, False).T
    down_out = lax.psum_scatter(down_sum, "section", scatter_dimension=0, tiled=True)
    down_out = lax.psum_scatter(down_out, "dp", scatter_dimension=1, tiled=True)
    gain_out = lax.psum_scatter(gain[:2], "section", scatter_dimension=0, tiled=True)
    gain_out = lax.psum_scatter(gain_out, "dp", scatter_dimension=1, tiled=True)
    return (stream_out, stream_grad, gain_out, first_out.astype(F32), down_out.astype(F32))


def solution(mesh):
    in_specs = (
        P(("dp", "section"), None),
        P("dp"),
        P("dp"),
        P("section", None),
        P("section", None, None),
        P("section", None),
        P(("dp", "section"), None),
    )
    out_specs = (
        P(("dp", "section"), None),
        P(("dp", "section"), None),
        P("section", "dp"),
        P("section", None, "dp"),
        P("section", "dp"),
    )
    return jax.shard_map(
        per_device, mesh=mesh, in_specs=in_specs, out_specs=out_specs, check_vma=False
    )
```

```python
import functools

import jax
import jax.numpy as jnp
from jax import lax
from jax.experimental import pallas as pl
from jax.experimental.pallas import tpu as pltpu
from jax.sharding import PartitionSpec as P

HEADS = 12
HEAD_DIM = 64
EPSILON = 1e-05
MASKED_SCORE = -1e30
LANE = 128
TILE = 256
F32 = jnp.float32
BF16 = jnp.bfloat16
VMEM_LIMIT = 66000000


def dot(left, right):
    return lax.dot_general(left, right, (((1,), (0,)), ((), ())), preferred_element_type=F32)


def dot_rows(left, right):
    return lax.dot_general(left, right, (((1,), (1,)), ((), ())), preferred_element_type=F32)


def dot_cols(left, right):
    return lax.dot_general(left, right, (((0,), (0,)), ((), ())), preferred_element_type=F32)


def lane_of(shape):
    return lax.broadcasted_iota(jnp.int32, shape, 1)


def padded(block):
    return jnp.pad(block.astype(F32), ((0, 0), (0, 1)))


def full_width(block):
    lane = lane_of(block.shape)
    last = block.shape[1] - 1
    kept = jnp.where(lane == last, 0.0, block)
    return jnp.where(lane == last, -jnp.sum(kept, axis=-1, keepdims=True), kept)


def norm_parts(block):
    full = full_width(block)
    scale = lax.rsqrt(jnp.mean(full * full, axis=-1, keepdims=True) + EPSILON)
    return full * scale, scale


def norm_back(fhat, scale, gain, grad):
    weighted = grad * gain
    inner = jnp.mean(weighted * fhat, axis=-1, keepdims=True)
    error = scale * (weighted - fhat * inner)
    last = error.shape[1] - 1
    tail = jnp.sum(jnp.where(lane_of(error.shape) == last, error, 0.0), axis=-1, keepdims=True)
    return error - tail


def drop_last(block):
    return jnp.where(lane_of(block.shape) == block.shape[1] - 1, 0.0, block)


def widen(block):
    return block - jnp.sum(block, axis=-1, keepdims=True) * (1.0 / block.shape[1])


def allowed_of(query_pos, key_pos, length, live_count):
    start = query_pos & (-length)
    usable = (key_pos < live_count) | (key_pos == query_pos)
    return (key_pos >= start) & (key_pos <= query_pos) & usable


MESH = pl.DeviceIdType.MESH
HALF = 384
PART = 192
GROUP = 48


class Refs:
    def __init__(self, **refs):
        self.__dict__.update(refs)


def scratch_of(rows, width, reduce):
    vmem = pltpu.VMEM
    dma = pltpu.SemaphoreType.DMA
    credit = pltpu.SemaphoreType.REGULAR
    shapes = dict(
        xs=vmem((rows, width - 1), BF16),
        ogs=vmem((rows, width - 1), BF16),
        wbuf=vmem((2, 4, width, width), BF16),
        w2=vmem((3, 8, LANE, width), BF16),
        gains=vmem((2, 1, width), F32),
        qkv=vmem((6, 3, rows, LANE), BF16),
        attnt=vmem((width, rows), BF16),
        mid=vmem((rows, width), BF16),
        nrm=vmem((rows, width), BF16),
        wide=vmem((rows, width), BF16),
        nt=vmem((width, rows), BF16),
        wt=vmem((width, rows), BF16),
        n1t=vmem((width, rows), BF16),
        act=vmem((rows, 8 * LANE), BF16),
        dpre=vmem((rows, 8 * LANE), BF16),
        br=vmem((rows, width), F32),
        dn=vmem((rows, width), F32),
        bias=vmem((rows, rows), BF16),
        vt=vmem((LANE, rows), BF16),
        lse=vmem((16, rows), F32),
        do=vmem((2, rows, LANE), BF16),
        dqt=vmem((LANE, rows), F32),
        gg=vmem((2, 8, width), F32),
        gbig=vmem((8, width, LANE), BF16),
        gdown=vmem((8, width, LANE), BF16),
        load_sem=dma((10,)),
        out_sem=dma((5,)),
        ga_send=dma((8, 9)),
        ga_recv=dma((8, 9)),
    )
    if reduce:
        shapes.update(
            g_rc=vmem((8, HALF, LANE), BF16),
            g_keep=vmem((4, HALF, LANE), BF16),
            g_s1=vmem((4, HALF, LANE), BF16),
            g_r2=vmem((2, 4, HALF, LANE), BF16),
            g_s2=vmem((2, 3, HALF, LANE), BF16),
            g_own=vmem((2, HALF, LANE), BF16),
            g_rz=vmem((2, 3, HALF, LANE), BF16),
            g_sx=vmem((HALF, LANE), BF16),
            g_rx=vmem((3, HALF, LANE), BF16),
            g_acc=vmem((3, width, LANE), F32),
            d_rc=vmem((8, HALF, LANE), BF16),
            d_keep=vmem((4, HALF, LANE), BF16),
            d_s1=vmem((4, HALF, LANE), BF16),
            d_r2=vmem((2, 4, HALF, LANE), BF16),
            d_keep2=vmem((4, PART, LANE), BF16),
            d_s2=vmem((4, PART, LANE), BF16),
            d_ry=vmem((2, 4, PART, LANE), BF16),
            d_s3=vmem((3, 4, GROUP, LANE), BF16),
            d_own=vmem((4, GROUP, LANE), BF16),
            d_rz=vmem((2, 3, 4, GROUP, LANE), BF16),
            d_acc=vmem((3, 4, GROUP, LANE), F32),
            n_sum=vmem((8, width), F32),
            n_send=vmem((4, 8, width), F32),
            n_recv=vmem((6, 8, width), F32),
            core_sem=dma((2, 2)),
            gy_send=dma((4,)),
            gy_recv=dma((2, 4)),
            gz_send=dma((2, 3)),
            gz_recv=dma((2, 3)),
            x_sem=dma((4,)),
            dx_sem=dma((3,)),
            dy_sem=dma((3,)),
            dz_send=dma((3,)),
            dz_recv=dma((2, 3)),
            n_sem=dma((2, 6)),
            end_sem=dma((2, 3)),
            credit=credit((6,)),
            z_credit=credit((2, 3)),
        )
    return shapes


class Place:
    def __init__(self):
        self.dp = lax.axis_index("dp")
        self.section = lax.axis_index("section")
        self.core = self.dp % 2
        self.y = (self.dp // 2) % 2
        self.z = self.dp // 4
        self.pair = (self.dp // 4) % 2
        self.pair_id = {"dp": self.dp + 4 - 8 * self.pair}
        self.core_id = {"dp": self.dp + 1 - 2 * self.core}
        self.y_id = {"dp": self.dp + 2 - 4 * self.y}
        self.x_id = {"section": 1 - self.section}

    def z_of(self, r):
        return (self.z + r) % 4

    def z_back(self, r):
        return (self.z + 4 - r) % 4

    def z_id(self, r):
        return {"dp": self.dp + 4 * (self.z_of(r) - self.z)}

    def z_back_id(self, r):
        return {"dp": self.dp + 4 * (self.z_back(r) - self.z)}


def remote(source, target, send_sem, recv_sem, device):
    return pltpu.make_async_remote_copy(
        src_ref=source, dst_ref=target, send_sem=send_sem, recv_sem=recv_sem,
        device_id=device, device_id_type=MESH,
    )


def landed(target, send_sem, recv_sem, device):
    remote(target, target, send_sem, recv_sem, device).wait_recv()


def sent(source, send_sem, recv_sem, device):
    remote(source, source, send_sem, recv_sem, device).wait_send()


class Gather:
    def __init__(self, refs, place):
        self.refs, self.place = refs, place
        self.mine, self.theirs = place.section, 1 - place.section

    def block(self, slot, piece, part):
        kind, k = piece
        if kind == "down":
            size = LANE // 2
            rows = pl.ds(pl.multiple_of(size * (part % 2), size), size)
            return self.refs.w2.at[k, 4 * slot + part // 2, rows, :], k + 5
        size = PART // 2
        rows = pl.ds(pl.multiple_of(size * part, size), size)
        if kind == "start":
            return self.refs.wbuf.at[slot, 0, rows, pl.ds(HALF * k, HALF)], k
        return self.refs.wbuf.at[slot, k, rows, :], k + 1

    def part(self, z, y, core):
        return 4 * z + 2 * y + core

    def copy(self, kind, piece, slot, part, device):
        ref, at = self.block(slot, piece, part)
        return remote(ref, ref, self.refs.ga_send.at[kind, at], self.refs.ga_recv.at[kind, at], device)

    def routes(self, piece, core):
        p = self.place
        own = self.part(p.pair, p.y, core)
        from_y = self.part(p.pair, 1 - p.y, core)
        from_z = self.part(1 - p.pair, p.y, core)
        far = self.part(1 - p.pair, 1 - p.y, core)
        return own, from_y, from_z, far

    def send_x(self, piece):
        own = self.routes(piece, self.place.core)[0]
        self.copy(0, piece, self.mine, own, self.place.x_id).start()

    def across(self, piece, part):
        p = self.place
        device = {"dp": p.dp + p.core * (2 - 4 * p.y) + (1 - p.core) * (4 - 8 * p.pair)}
        return self.copy(3, piece, self.theirs, part, device)

    def forward(self, piece):
        p = self.place
        own = self.routes(piece, p.core)[0]
        self.copy(0, piece, self.theirs, own, p.x_id).wait_recv()
        self.copy(1, piece, self.theirs, own, p.y_id).start()
        self.copy(2, piece, self.theirs, own, p.pair_id).start()
        self.copy(4, piece, self.theirs, own, p.core_id).start()

    def relay(self, piece):
        p = self.place
        _, from_y, from_z, _ = self.routes(piece, p.core)
        self.copy(1, piece, self.theirs, from_y, p.y_id).wait_recv()
        self.copy(5, piece, self.theirs, from_y, p.core_id).start()
        self.copy(2, piece, self.theirs, from_z, p.pair_id).wait_recv()
        self.copy(6, piece, self.theirs, from_z, p.core_id).start()
        self.across(piece, p.core * from_z + (1 - p.core) * from_y).start()

    def close(self, piece):
        p = self.place
        far = self.routes(piece, p.core)[3]
        self.across(piece, far).wait_recv()
        self.copy(7, piece, self.theirs, far, p.core_id).start()

    def use(self, piece):
        p = self.place
        for kind, part in enumerate(self.routes(piece, 1 - p.core)):
            self.copy(4 + kind, piece, self.theirs, part, p.core_id).wait_recv()

    def drain(self, piece):
        p = self.place
        own, from_y, from_z, far = self.routes(piece, p.core)
        self.copy(0, piece, self.mine, own, p.x_id).wait_send()
        self.copy(1, piece, self.theirs, own, p.y_id).wait_send()
        self.copy(2, piece, self.theirs, own, p.pair_id).wait_send()
        self.across(piece, p.core * from_z + (1 - p.core) * from_y).wait_send()
        for kind, part in enumerate((own, from_y, from_z, far)):
            self.copy(4 + kind, piece, self.theirs, part, p.core_id).wait_send()


START = [("start", k) for k in range(2)]
FIRST = [("first", k) for k in range(1, 4)]
DOWN = [("down", k) for k in range(3)]


def half_rows(half):
    return pl.ds(pl.multiple_of(HALF * half, HALF), HALF)


def when(condition, action):
    if isinstance(condition, bool):
        if condition:
            action()
    else:
        pl.when(condition)(action)


class BigSum:
    jobs = 6

    def __init__(self, refs, place):
        self.r, self.p = refs, place

    def core_copy(self):
        r, p = self.r, self.p
        return remote(
            r.gbig.at[:, half_rows(1 - p.core), :], r.g_rc, r.core_sem.at[0, 0], r.core_sem.at[1, 0], p.core_id
        )

    def start(self, j):
        when(j >= 1, lambda: pl.semaphore_wait(self.r.credit.at[0], 1))
        self.core_copy().start()

    def y_copy(self, j, block):
        r, p = self.r, self.p
        return remote(
            r.g_s1.at[block], r.g_r2.at[j % 2, block], r.gy_send.at[block], r.gy_recv.at[j % 2, block], p.y_id
        )

    def after_core(self, j):
        r, p = self.r, self.p
        self.core_copy().wait()
        own = half_rows(p.core)
        when(j >= 2, lambda: pl.semaphore_wait(r.credit.at[1], 1))
        for k in range(4):
            z = p.z_of((k + 1) % 4)
            at = 4 * (1 - p.y) + z
            r.g_s1[z] = r.gbig[at, own, :] + r.g_rc[at]
            self.y_copy(j, z).start()
        for z in range(4):
            at = 4 * p.y + z
            r.g_keep[z] = r.gbig[at, own, :] + r.g_rc[at]
        when(
            j <= self.jobs - 2,
            lambda: pl.semaphore_signal(r.credit.at[0], inc=1, device_id=p.core_id, device_id_type=MESH),
        )

    def z_copy(self, j, k):
        r, p = self.r, self.p
        return remote(
            r.g_s2.at[j % 2, k - 1], r.g_rz.at[j % 2, k - 1], r.gz_send.at[j % 2, k - 1], r.gz_recv.at[j % 2, k - 1], p.z_id(k)
        )

    def after_y(self, j):
        r, p = self.r, self.p
        slot = j % 2
        for k in range(1, 4):
            z = p.z_of(k)
            self.y_copy(j, z).wait_recv()
            r.g_s2[slot, k - 1] = r.g_keep[z] + r.g_r2[slot, z]
            when(j >= 2, lambda k=k: pl.semaphore_wait(r.z_credit.at[0, k - 1], 1))
            self.z_copy(j, k).start()
        self.y_copy(j, p.z).wait_recv()
        r.g_own[slot] = r.g_keep[p.z] + r.g_r2[slot, p.z]
        for k in range(4):
            self.y_copy(j, k).wait_send()
        when(
            j <= self.jobs - 3,
            lambda: pl.semaphore_signal(r.credit.at[1], inc=1, device_id=p.y_id, device_id_type=MESH),
        )

    def x_copy(self, chunk):
        r, p = self.r, self.p
        return remote(r.g_sx, r.g_rx.at[chunk], r.x_sem.at[3], r.x_sem.at[chunk], p.x_id)

    def after_z(self, j, chunk, target):
        r, p = self.r, self.p
        slot = j % 2
        for k in range(1, 4):
            self.z_copy(j, k).wait()
        total = r.g_own[slot].astype(F32)
        for k in range(3):
            total = total + r.g_rz[slot, k].astype(F32)

        @pl.when(p.section != target)
        def _():
            r.g_sx[...] = total.astype(BF16)
            self.x_copy(chunk).start()

        @pl.when(p.section == target)
        def _():
            r.g_acc[chunk, half_rows(p.core), :] = total

        for k in range(1, 4):
            when(
                j <= self.jobs - 3,
                lambda k=k: pl.semaphore_signal(
                    r.z_credit.at[0, k - 1], inc=1, device_id=p.z_back_id(k), device_id_type=MESH
                ),
            )

    def after_x(self, chunk, target):
        r, p = self.r, self.p

        @pl.when(p.section != target)
        def _():
            self.x_copy(chunk).wait_send()

        @pl.when(p.section == target)
        def _():
            self.x_copy(chunk).wait_recv()
            own = half_rows(p.core)
            r.g_acc[chunk, own, :] = r.g_acc[chunk, own, :] + r.g_rx[chunk].astype(F32)


class DownSum:
    jobs = 3

    def __init__(self, refs, place):
        self.r, self.p = refs, place

    def core_copy(self):
        r, p = self.r, self.p
        return remote(
            r.gdown.at[:, half_rows(1 - p.core), :], r.d_rc, r.core_sem.at[0, 1], r.core_sem.at[1, 1], p.core_id
        )

    def start(self, j):
        when(j >= 1, lambda: pl.semaphore_wait(self.r.credit.at[2], 1))
        self.core_copy().start()

    def x_copy(self, j):
        r, p = self.r, self.p
        return remote(r.d_s1, r.d_r2.at[j % 2], r.dx_sem.at[2], r.dx_sem.at[j % 2], p.x_id)

    def after_core(self, j):
        r, p = self.r, self.p
        self.core_copy().wait()
        own = half_rows(p.core)
        for k in range(4):
            at = 4 * (1 - p.section) + k
            r.d_s1[k] = r.gdown[at, own, :] + r.d_rc[at]
        when(j >= 2, lambda: pl.semaphore_wait(r.credit.at[3], 1))
        self.x_copy(j).start()
        for k in range(4):
            at = 4 * p.section + k
            r.d_keep[k] = r.gdown[at, own, :] + r.d_rc[at]
        when(
            j <= self.jobs - 2,
            lambda: pl.semaphore_signal(r.credit.at[2], inc=1, device_id=p.core_id, device_id_type=MESH),
        )

    def y_copy(self, j):
        r, p = self.r, self.p
        return remote(r.d_s2, r.d_ry.at[j % 2], r.dy_sem.at[2], r.dy_sem.at[j % 2], p.y_id)

    def after_x(self, j):
        r, p = self.r, self.p
        slot = j % 2
        self.x_copy(j).wait()
        theirs = pl.ds(pl.multiple_of(PART * (1 - p.y), PART), PART)
        mine = pl.ds(pl.multiple_of(PART * p.y, PART), PART)
        for k in range(4):
            r.d_s2[k] = r.d_keep[k, theirs, :] + r.d_r2[slot, k, theirs, :]
        when(j >= 2, lambda: pl.semaphore_wait(r.credit.at[4], 1))
        self.y_copy(j).start()
        for k in range(4):
            r.d_keep2[k] = r.d_keep[k, mine, :] + r.d_r2[slot, k, mine, :]
        when(
            j <= self.jobs - 3,
            lambda: pl.semaphore_signal(r.credit.at[3], inc=1, device_id=p.x_id, device_id_type=MESH),
        )

    def z_copy(self, j, k):
        r, p = self.r, self.p
        return remote(
            r.d_s3.at[k - 1], r.d_rz.at[j % 2, k - 1], r.dz_send.at[k - 1], r.dz_recv.at[j % 2, k - 1], p.z_id(k)
        )

    def after_y(self, j):
        r, p = self.r, self.p
        slot = j % 2
        self.y_copy(j).wait()
        for k in range(4):
            rows = pl.ds(pl.multiple_of(GROUP * p.z_of(k), GROUP), GROUP)
            for f in range(4):
                total = r.d_keep2[f, rows, :] + r.d_ry[slot, f, rows, :]
                if k == 0:
                    r.d_own[f] = total
                else:
                    r.d_s3[k - 1, f] = total
        for k in range(1, 4):
            when(j >= 2, lambda k=k: pl.semaphore_wait(r.z_credit.at[1, k - 1], 1))
            self.z_copy(j, k).start()
        when(
            j <= self.jobs - 3,
            lambda: pl.semaphore_signal(r.credit.at[4], inc=1, device_id=p.y_id, device_id_type=MESH),
        )

    def after_z(self, j):
        r, p = self.r, self.p
        slot = j % 2
        for k in range(1, 4):
            self.z_copy(j, k).wait()
        for f in range(4):
            total = r.d_own[f].astype(F32)
            for k in range(3):
                total = total + r.d_rz[slot, k, f].astype(F32)
            r.d_acc[j, f] = total
        for k in range(1, 4):
            when(
                j <= self.jobs - 3,
                lambda k=k: pl.semaphore_signal(
                    r.z_credit.at[1, k - 1], inc=1, device_id=p.z_back_id(k), device_id_type=MESH
                ),
            )


class NormSum:
    def __init__(self, refs, place):
        self.r, self.p = refs, place

    def copy(self, stage, slot, device):
        r = self.r
        return remote(
            r.n_send.at[stage], r.n_recv.at[slot], r.n_sem.at[0, slot], r.n_sem.at[1, slot], device
        )

    def routes(self, stage):
        p = self.p
        return [
            [(0, p.core_id)], [(1, p.y_id)], [(2, p.z_id(1)), (3, p.z_id(2)), (4, p.z_id(3))], [(5, p.x_id)]
        ][stage]

    def send(self, stage):
        r = self.r
        r.n_send[stage] = r.n_sum[...]
        for slot, device in self.routes(stage):
            self.copy(stage, slot, device).start()

    def receive(self, stage):
        r = self.r
        for slot, device in self.routes(stage):
            self.copy(stage, slot, device).wait()
            r.n_sum[...] += r.n_recv[slot]


def layer_kernel(reduce, names, length_ref, live_ref, x_hbm, og_hbm, gain_in, first_hbm, down_hbm, out_hbm, grad_hbm, *rest):
    outs = rest[:3]
    r = Refs(**dict(zip(names, rest[3:])))
    place = Place()
    rows, width = r.mid.shape
    tiles = rows // TILE
    section = place.section
    length, live_count = length_ref[0], live_ref[0] - section * rows
    gather = Gather(r, place)
    big, down, norms = BigSum(r, place), DownSum(r, place), NormSum(r, place)

    def tile_at(tile):
        return pl.ds(pl.multiple_of(tile * TILE, TILE), TILE)

    def wide_at(tile):
        return pl.ds(pl.multiple_of(tile * 2 * TILE, 2 * TILE), 2 * TILE)

    def lane_at(lo):
        return pl.ds(pl.multiple_of(lo, LANE), LANE)

    def load(source, target, index):
        return pltpu.make_async_copy(source, target, r.load_sem.at[index])

    barrier = pltpu.get_barrier_semaphore()
    greeted = [place.core_id, place.y_id, place.x_id]
    greeted += [place.z_id(k) for k in range(1, 4)] if reduce else [place.pair_id]
    for device in greeted:
        pl.semaphore_signal(barrier, inc=1, device_id=device, device_id_type=MESH)
    x_load = load(x_hbm, r.xs, 7)
    og_load = load(og_hbm, r.ogs, 8)
    gain_load = load(gain_in, r.gains.at[section], 9)
    gain_load.start()
    for k in range(3):
        for z in range(3):
            for y in range(2):
                lo = width * z + HALF * y + LANE * k
                load(
                    first_hbm.at[:, pl.ds(lo, LANE)],
                    r.wbuf.at[section, k, :, pl.ds((3 * y + z) * LANE, LANE)],
                    k,
                ).start()
        if k == 0:
            x_load.start()
    load(first_hbm.at[:, pl.ds(3 * width, width)], r.wbuf.at[section, 3], 3).start()
    og_load.start()
    for k in range(3):
        for z in range(2):
            for y in range(2):
                lo = width * z + HALF * y + LANE * k
                load(
                    down_hbm.at[pl.ds(lo, LANE), :], r.w2.at[k, 4 * section + 2 * z + y], 4 + k
                ).start()

    gain_load.wait()
    pl.semaphore_wait(barrier, len(greeted))

    gain_ref = r.gains.at[section]
    gain_copy = remote(gain_ref, gain_ref, r.ga_send.at[0, 8], r.ga_recv.at[0, 8], place.x_id)
    gain_copy.start()
    for k in range(4):
        load(r.wbuf.at[section, k], r.wbuf.at[section, k], k).wait()
        for piece in START if k == 0 else [("first", k)]:
            gather.send_x(piece)
    for k in range(3):
        mine = r.w2.at[k, pl.ds(4 * section, 4)]
        load(mine, mine, 4 + k).wait()
        gather.send_x(("down", k))
    og_load.wait()

    def live_of(tile):
        row = tile * TILE + lax.broadcasted_iota(jnp.int32, (TILE, 1), 0)
        return (row < live_count).astype(F32)

    for tile in range(tiles):
        at = tile_at(tile)
        out_live = padded(r.ogs[at, :]) * live_of(tile)
        wide = widen(out_live).astype(BF16)
        r.wide[at, :] = wide
        turned = wide.T
        if reduce:
            for z in range(4):
                for y in range(2):
                    for c in range(2):
                        lo = PART * z + 2 * GROUP * y + GROUP * c
                        to = HALF * c + PART * y + GROUP * z
                        r.wt[pl.ds(to, GROUP), at] = turned[lo : lo + GROUP, :]
        else:
            r.wt[:, at] = turned

    def mask_step(tile, carry):
        at = tile_at(tile)
        key = tile * TILE + lax.broadcasted_iota(jnp.int32, (TILE, rows), 0)
        query = lax.broadcasted_iota(jnp.int32, (TILE, rows), 1)
        allowed = allowed_of(query, key, length, live_count)
        r.bias[at, :] = jnp.where(allowed, 0.0, MASKED_SCORE).astype(BF16)
        return carry

    lax.fori_loop(0, tiles, mask_step, 0)
    x_load.wait()
    theirs = r.gains.at[1 - section]
    landed(theirs, r.ga_send.at[0, 8], r.ga_recv.at[0, 8], place.x_id)
    gather.forward(START[0])

    def begin_step(tile, carry):
        at = tile_at(tile)
        fhat, _ = norm_parts(padded(r.xs[at, :]))
        norm = (fhat * r.gains[0]).astype(BF16)
        r.nrm[at, :] = norm
        r.n1t[:, at] = norm.T
        return carry

    lax.fori_loop(0, tiles, begin_step, 0)
    gather.forward(START[1])
    gather.relay(START[0])
    gather.forward(FIRST[0])
    gather.relay(START[1])
    gather.close(START[0])

    def project_half(y):
        lanes = pl.ds(HALF * y, HALF)

        pl.when(section == 1)(lambda: gather.use(START[y]))

        def project(tile, inner):
            at = wide_at(tile)
            out = dot(r.nrm[at, :], r.wbuf[0, 0, :, lanes]).astype(BF16)
            for t in range(3):
                r.qkv[y, t, at, :] = out[:, t * LANE : (t + 1) * LANE]
            return inner

        lax.fori_loop(0, tiles // 2, project, 0)

    def attention_step(p, carry):
        def project(tile, inner):
            at = wide_at(tile)
            out = dot(r.nrm[at, :], r.wbuf[0, p]).astype(BF16)
            for t in range(3):
                for y in range(2):
                    lo = (3 * y + t) * LANE
                    r.qkv[2 * p + y, t, at, :] = out[:, lo : lo + LANE]
            return inner

        @pl.when(p >= 1)
        def _():
            lax.fori_loop(0, tiles // 2, project, 0)

        def pair(y, inner):
            block = 2 * p + y
            first_head = 6 * y + 2 * p

            turn = 2 * p + y

            def at_turn(number, *actions):
                @pl.when(turn == number)
                def _():
                    for action, argument in actions:
                        action(argument)

            first, second, third = FIRST
            at_turn(
                0,
                (project_half, 0),
                (gather.close, START[1]),
                (gather.relay, first),
                (gather.forward, second),
            )
            at_turn(1, (project_half, 1))
            at_turn(2, (gather.relay, second), (gather.forward, third))
            at_turn(4, (gather.relay, third))
            r.vt[...] = r.qkv[block, 2].T
            out_rows = pl.multiple_of(HALF * y + LANE * p, LANE)

            def scores_of(qb, i):
                count = (qb + 1) * TILE
                at = pl.ds(qb * TILE, TILE)
                lane = lane_of((TILE, LANE))
                mine = (lane < HEAD_DIM) if i == 0 else (lane >= HEAD_DIM)
                query = jnp.where(mine, r.qkv[block, 0, at, :] * BF16(HEAD_DIM**-0.5), BF16(0))
                keys = r.qkv[block, 1, pl.ds(0, count), :]
                return dot_rows(keys, query) + r.bias[pl.ds(0, count), at].astype(F32)

            def mix(qb, i, scores):
                count = (qb + 1) * TILE
                at = pl.ds(qb * TILE, TILE)
                top = jnp.max(scores, axis=0, keepdims=True)
                terms = jnp.exp(scores - top).astype(BF16)
                values = jnp.concatenate(
                    [r.vt[pl.ds(i * HEAD_DIM, HEAD_DIM), pl.ds(0, count)], jnp.ones((16, count), BF16)], 0
                )
                out = dot(values, terms)
                total = out[HEAD_DIM : HEAD_DIM + 1, :]
                r.lse[pl.ds(first_head + i, 1), at] = top + jnp.log(total)
                r.attnt[pl.ds(out_rows + i * HEAD_DIM, HEAD_DIM), at] = (
                    out[:HEAD_DIM, :] / total
                ).astype(BF16)

            waiting = None
            for qb in range(tiles):
                for i in range(2):
                    scores = scores_of(qb, i)
                    if waiting is not None:
                        mix(*waiting)
                    waiting = (qb, i, scores)
            mix(*waiting)
            at_turn(1, (gather.close, first))
            at_turn(3, (gather.close, second), (gather.forward, DOWN[0]))
            at_turn(5, (gather.close, third), (gather.relay, DOWN[0]), (gather.forward, DOWN[1]))
            return inner

        lax.fori_loop(0, 2, pair, 0)
        pl.when(section == 1)(lambda: gather.use(("first", p + 1)))
        return carry

    lax.fori_loop(0, 3, attention_step, 0)

    def attention_end(tile, carry):
        at = wide_at(tile)
        branch = dot_cols(r.attnt[:, at], r.wbuf[0, 3])
        mean = jnp.sum(branch, axis=-1, keepdims=True) * (1.0 / width)
        mid = drop_last(padded(r.xs[at, :]) + branch - mean).astype(BF16)
        r.mid[at, :] = mid
        fhat, _ = norm_parts(mid.astype(F32))
        norm = (fhat * r.gains[1]).astype(BF16)
        r.nrm[at, :] = norm
        r.nt[:, at] = norm.T
        return carry

    for tile in range(tiles // 2):
        attention_end(tile, 0)

    gather.close(DOWN[0])
    gather.forward(DOWN[2])

    @pl.when(section == 0)
    def _():
        for piece in START + FIRST:
            gather.use(piece)

    r.br[...] = jnp.zeros_like(r.br)
    r.dn[...] = jnp.zeros_like(r.dn)

    def dump(source, output, chunk, index):
        copy = pltpu.make_async_copy(source, output.at[chunk], r.out_sem.at[index])
        copy.start()
        copy.wait()

    def mlp_end(first_row, count):
        at = pl.ds(pl.multiple_of(first_row, count), count)
        row = first_row + lax.broadcasted_iota(jnp.int32, (count, 1), 0)
        live = (row < live_count).astype(F32)
        mid = r.mid[at, :].astype(F32)
        out_live = padded(r.ogs[at, :]) * live
        branch = r.br[at, :]
        mean = jnp.sum(branch, axis=-1, keepdims=True) * (1.0 / width)
        out = ((mid + branch - mean) * live).astype(BF16)
        r.ogs[at, :] = out[:, : width - 1]
        fhat, scale = norm_parts(mid)
        grad = r.dn[at, :]
        back = norm_back(fhat, scale, r.gains[1], grad)
        r.gg[1] += jnp.sum((grad * fhat).reshape(count // 8, 8, width), axis=0)
        d_mid = drop_last(out_live + back).astype(BF16)
        r.mid[at, :] = d_mid
        r.wide[at, :] = widen(d_mid.astype(F32)).astype(BF16)

    r.gg[...] = jnp.zeros_like(r.gg)

    def mlp_step(p, carry, last):
        gather.use(("down", p))

        def first_columns(n):
            if n < 3:
                return jnp.concatenate(
                    [r.wbuf[1, p, :, pl.ds((3 * y + n) * LANE, LANE)] for y in range(2)], 1
                )
            return jnp.concatenate(
                [r.wbuf[1, 3, :, lane_at(HALF * y + LANE * p)] for y in range(2)], 1
            )

        def hidden(tile, n):
            at = wide_at(tile)
            col = pl.ds(n * TILE, TILE)
            pre = dot(r.nrm[at, :], first_columns(n))
            d_act = dot_rows(r.wide[at, :], r.w2[p, pl.ds(2 * n, 2)].reshape(TILE, width))
            square = pre * pre
            inner_arg = pre * (0.7978845608028654 + (0.044715 * 0.7978845608028654) * square)
            tanh = jnp.tanh(inner_arg)
            half = 0.5 + 0.5 * tanh
            slope = half + (0.5 * pre) * (1.0 - tanh * tanh) * (
                0.7978845608028654 + (3.0 * 0.044715 * 0.7978845608028654) * square
            )
            r.act[at, col] = (pre * half).astype(BF16)
            r.dpre[at, col] = (d_act * slope).astype(BF16)

        def branch_part(tile, m):
            at = wide_at(tile)
            col = pl.ds(m * TILE, TILE)
            w2 = r.w2[p, :, :, col].reshape(8 * LANE, TILE)
            r.br[at, col] += dot(r.act[at, :], w2)

        def norm_part(tile, m):
            at = wide_at(tile)
            col = pl.ds(m * TILE, TILE)
            w1 = jnp.concatenate(
                [
                    r.wbuf[1, p, col, pl.ds((3 * y + z) * LANE, LANE)]
                    for z in range(3)
                    for y in range(2)
                ]
                + [r.wbuf[1, 3, col, lane_at(HALF * y + LANE * p)] for y in range(2)],
                1,
            )
            r.dn[at, col] += dot_rows(r.dpre[at, :], w1)

        for n in range(4):
            hidden(0, n)
        when(p == 0, lambda: gather.relay(DOWN[1]))

        def rows_step(tile, inner):
            for n in range(4):
                hidden(tile, n)
                if n < 3:
                    branch_part(tile - 1, n)
                    norm_part(tile - 1, n)
            return inner

        for tile in range(1, tiles // 2):
            rows_step(tile, 0)
        for n in range(3):
            branch_part(tiles // 2 - 1, n)
            norm_part(tiles // 2 - 1, n)

        def pass_on():
            gather.close(DOWN[1])
            gather.relay(DOWN[2])

        when(p == 0, pass_on)

        def ends(step, k):
            if last:
                size = rows // 16
                mlp_end(step * (rows // 2) + k * size, size)

        def grads(half, step):
            own = half_rows(half)
            for n in range(4):
                g1 = dot(r.nt[own, :], r.dpre[:, pl.ds(n * TILE, TILE)]).astype(BF16)
                ends(step, n)
                for y in range(2):
                    r.gbig[4 * y + n, own, :] = g1[:, y * LANE : (y + 1) * LANE]

        def down_grads(half, step):
            own = half_rows(half)
            for n in range(4):
                g2 = dot(r.wt[own, :], r.act[:, pl.ds(n * TILE, TILE)]).astype(BF16)
                ends(step, n + 4)
                for y in range(2):
                    r.gdown[2 * n + y, own, :] = g2[:, y * LANE : (y + 1) * LANE]

        def half_step(step, inner):
            if not reduce:
                grads(step, step)
                down_grads(step, step)
                return inner
            half = (1 - place.core) * (1 - step) + place.core * step
            grads(half, step)
            pl.when(step == 0)(lambda: big.start(p))
            down_grads(half, step)
            pl.when(step == 0)(lambda: down.start(p))
            return inner

        lax.fori_loop(0, 2, half_step, 0)
        if reduce:

            def older():
                big.after_z(0, 0, 1)
                down.after_y(0)

            def old():
                big.after_y(p - 1)
                down.after_x(p - 1)

            when(p == 2, older)
            when(p >= 1, old)
            big.after_core(p)
            down.after_core(p)
            when(p == 0, lambda: gather.close(DOWN[2]))
        if not reduce:
            when(p == 0, lambda: gather.close(DOWN[2]))
            dump(r.gbig, outs[1], p, 0)
            dump(r.gdown, outs[2], p, 1)
        return carry

    lax.fori_loop(0, 2, lambda p, carry: mlp_step(p, carry, False), 0)
    mlp_step(2, 0, True)
    out_store = pltpu.make_async_copy(r.ogs, out_hbm, r.out_sem.at[2])
    out_store.start()
    for piece in START + FIRST + DOWN:
        gather.drain(piece)
    gain_copy.wait_send()

    def back_step(p, carry):
        def project(tile, inner):
            at = wide_at(tile)
            wo = jnp.concatenate(
                [r.wbuf[0, 3, lane_at(HALF * y + LANE * p), :] for y in range(2)], 0
            )
            out = dot_rows(r.wide[at, :], wo).astype(BF16)
            r.do[0, at, :] = out[:, :LANE]
            r.do[1, at, :] = out[:, LANE:]
            return inner

        lax.fori_loop(0, tiles // 2, project, 0)

        def pair(y, inner):
            block = 2 * p + y
            first_head = 6 * y + 2 * p
            attn_rows = pl.ds(pl.multiple_of(HALF * y + LANE * p, LANE), LANE)
            product = r.do[y].T.astype(F32) * r.attnt[attn_rows, :].astype(F32)
            dots = [
                jnp.sum(product[i * HEAD_DIM : (i + 1) * HEAD_DIM, :], axis=0, keepdims=True)
                for i in range(2)
            ]
            lses = [r.lse[pl.ds(first_head + i, 1), :] for i in range(2)]
            r.dqt[...] = jnp.zeros_like(r.dqt)
            for kb in range(tiles):
                lo = kb * TILE
                at = pl.ds(lo, TILE)
                rest = pl.ds(lo, rows - lo)
                lane = lane_of((TILE, LANE))
                query = r.qkv[block, 0, rest, :] * BF16(HEAD_DIM**-0.5)
                keys = r.qkv[block, 1, at, :]
                values = r.qkv[block, 2, at, :]
                d_out = r.do[y, rest, :]
                bias = r.bias[at, rest].astype(F32)
                d_keys, d_values = [], []
                for i in range(2):
                    mine = (lane < HEAD_DIM) if i == 0 else (lane >= HEAD_DIM)
                    keys_mine = jnp.where(mine, keys, BF16(0))
                    scores = dot_rows(keys_mine, query) + bias
                    probs = jnp.exp(scores - lses[i][:, lo:])
                    d_probs = dot_rows(jnp.where(mine, values, BF16(0)), d_out)
                    d_scores = (probs * (d_probs - dots[i][:, lo:])).astype(BF16)
                    d_values.append(dot(probs.astype(BF16), d_out))
                    d_keys.append(dot(d_scores, query))
                    r.dqt[:, rest] += dot(keys_mine.T, d_scores)
                for t, parts in ((1, d_keys), (2, d_values)):
                    whole = jnp.where(lane < HEAD_DIM, parts[0], parts[1]).astype(BF16)
                    r.w2[p, pl.ds(2 * kb, 2), :, lane_at((3 * y + t) * LANE)] = whole.reshape(2, LANE, LANE)
            d_query = (r.dqt[...] * HEAD_DIM**-0.5).T.astype(BF16)
            r.w2[p, :, :, lane_at(3 * y * LANE)] = d_query.reshape(8, LANE, LANE)
            if reduce:

                @pl.when(jnp.logical_and(p == 0, y == 1))
                def _():
                    down.after_z(0)
                    down.after_y(1)
                    down.after_x(2)

                @pl.when(jnp.logical_and(p == 1, y == 0))
                def _():
                    down.after_z(1)
                    down.after_y(2)

                @pl.when(jnp.logical_and(p == 2, y == 1))
                def _():
                    down.after_z(2)

            return inner

        lax.fori_loop(0, 2, pair, 0)

        def grads(half):
            own = half_rows(half)
            for n in range(4):
                if n < 3:
                    d_qkv = jnp.concatenate(
                        [
                            r.w2[p, :, :, pl.ds((3 * y + n) * LANE, LANE)].reshape(rows, LANE)
                            for y in range(2)
                        ],
                        1,
                    )
                    out = dot(r.n1t[own, :], d_qkv).astype(BF16)
                else:
                    wide = jnp.concatenate(
                        [r.wide[:, lane_at(HALF * y + LANE * p)] for y in range(2)], 1
                    )
                    out = dot(r.attnt[own, :], wide).astype(BF16)
                for y in range(2):
                    r.gbig[4 * y + n, own, :] = out[:, y * LANE : (y + 1) * LANE]

        def half_step(step, inner):
            if not reduce:
                grads(step)
                return inner
            grads((1 - place.core) * (1 - step) + place.core * step)


            @pl.when(step == 0)
            def _():
                big.start(p + 3)
                big.after_y(p + 2)

            return inner

        lax.fori_loop(0, 2, half_step, 0)
        if reduce:
            big.after_x(p, 1)
            big.after_z(p + 1, jnp.where(p == 2, 0, p + 1), jnp.where(p == 2, 0, 1))
            big.after_core(p + 3)
        if not reduce:
            dump(r.gbig, outs[0], p, 0)

        return carry

    lax.fori_loop(0, 3, back_step, 0)

    def back_end(tile, carry):
        at = tile_at(tile)
        fhat, scale = norm_parts(padded(r.xs[at, :]))
        d_qkv = jnp.concatenate(
            [r.w2[p, pl.ds(2 * tile, 2)].reshape(TILE, width) for p in range(3)], 1
        )
        w_in = jnp.concatenate([r.wbuf[0, p] for p in range(3)], 1)
        grad = dot_rows(d_qkv, w_in)
        back = norm_back(fhat, scale, r.gains[0], grad)
        r.gg[0] += jnp.sum((grad * fhat).reshape(TILE // 8, 8, width), axis=0)
        r.xs[at, :] = (r.mid[at, :].astype(F32) + back).astype(BF16)[:, : width - 1]
        return carry

    lax.fori_loop(0, tiles, back_end, 0)
    grad_store = pltpu.make_async_copy(r.xs, grad_hbm, r.out_sem.at[3])
    grad_store.start()

    gg = [jnp.sum(r.gg[i], axis=0, keepdims=True) for i in range(2)]
    row = lax.broadcasted_iota(jnp.int32, (8, width), 0)
    gain_rows = jnp.where(row == 0, gg[0], 0.0) + jnp.where(row == 1, gg[1], 0.0)
    if reduce:
        r.n_sum[...] = gain_rows

        def end_copy(chunk, half):
            block = r.g_acc.at[chunk, half_rows(half), :]
            return remote(block, block, r.end_sem.at[0, chunk], r.end_sem.at[1, chunk], place.core_id)

        norms.send(0)
        big.after_y(5)
        norms.receive(0)
        norms.send(1)
        big.after_x(0, 0)
        end_copy(0, place.core).start()
        big.after_z(4, 1, 0)
        norms.receive(1)
        norms.send(2)
        big.after_x(1, 0)
        end_copy(1, place.core).start()
        big.after_z(5, 2, 0)
        norms.receive(2)
        norms.send(3)
        big.after_x(2, 0)
        end_copy(2, place.core).start()
        norms.receive(3)
        for chunk in range(3):
            end_copy(chunk, place.core).wait_send()
            end_copy(chunk, 1 - place.core).wait_recv()
        stores = [
            pltpu.make_async_copy(r.g_acc, outs[0], r.out_sem.at[0]),
            pltpu.make_async_copy(r.d_acc, outs[1], r.out_sem.at[1]),
            pltpu.make_async_copy(r.n_sum, outs[2], r.out_sem.at[4]),
        ]
        for store in stores:
            store.start()
        for store in stores:
            store.wait()
    out_store.wait()
    grad_store.wait()
    return gain_rows


def plain_kernel(names, *args):
    gain_out, rest = args[9], args[:9] + args[10:]
    gain_out[...] = layer_kernel(False, names, *rest)


def sum_kernel(names, *args):
    layer_kernel(True, names, *args)


def finish_kernel(out_hbm, grad_hbm, acc_hbm, down_hbm, gain_hbm, *rest):
    out_to, grad_to, gain_to, first_to, down_to = rest[:5]
    streams, acc, down, gain, first_out, down_out, sems = rest[5:]
    dp, section = lax.axis_index("dp"), lax.axis_index("section")
    core = dp % 2
    loads = [
        pltpu.make_async_copy(out_hbm, streams.at[0], sems.at[0]),
        pltpu.make_async_copy(grad_hbm, streams.at[1], sems.at[1]),
        pltpu.make_async_copy(acc_hbm, acc, sems.at[2]),
        pltpu.make_async_copy(down_hbm, down, sems.at[3]),
        pltpu.make_async_copy(gain_hbm, gain, sems.at[4]),
    ]
    for load in loads:
        load.start()
    stores = []

    def store(source, target, index):
        stores.append(pltpu.make_async_copy(source, target, sems.at[index]))
        stores[-1].start()

    for k, target in ((0, out_to), (1, grad_to)):
        loads[k].wait()
        store(streams.at[k], target, k)
    loads[2].wait()
    half = LANE // 2

    @pl.when(core == 0)
    def _():
        first_out[:LANE, :] = acc[0].T
        first_out[LANE:, :] = acc[1].T[:half, :]

    @pl.when(core == 1)
    def _():
        first_out[:half, :] = acc[1].T[half:, :]
        first_out[half:, :] = acc[2].T

    store(first_out, first_to, 2)
    loads[3].wait()
    for p in range(3):
        for k in range(4):
            lo = (k // 2) * 6 * LANE + (k % 2) * 3 * LANE + p * LANE
            down_out[:, pl.ds(lo, LANE)] = down[p, k]
    store(down_out, down_to, 3)
    loads[4].wait()
    width = gain.shape[1]
    share = gain_to.shape[1]
    row = lax.broadcasted_iota(jnp.int32, gain.shape, 0)
    mine = jnp.sum(jnp.where(row == section, gain[...], 0.0), axis=0, keepdims=True)
    turned = pltpu.roll(jnp.broadcast_to(mine, gain.shape), (width - dp * share) % width, 1)
    gain_to[...] = turned[:1, :share]
    for copy in stores:
        copy.wait()


def per_device(stream_in, seq_len, live_rows, norm_gain, first_weight, down_weight, out_grad):
    rows, width = stream_in.shape[0], norm_gain.shape[1]
    reduce = lax.axis_size("dp") == 16
    shapes = scratch_of(rows, width, reduce)
    names = tuple(shapes)
    anywhere = pl.BlockSpec(memory_space=pl.ANY)
    in_vmem = pl.BlockSpec(memory_space=pltpu.VMEM)
    stream = jax.ShapeDtypeStruct((rows, width - 1), BF16)
    gains = jax.ShapeDtypeStruct((8, width), F32)
    if reduce:
        outs = [
            jax.ShapeDtypeStruct((3, width, LANE), F32),
            jax.ShapeDtypeStruct((3, 4, GROUP, LANE), F32),
            gains,
        ]
        out_specs = [anywhere] * 3
        kernel = functools.partial(sum_kernel, names)
    else:
        chunks = jax.ShapeDtypeStruct((3, 8, width, LANE), BF16)
        outs = [gains, chunks, chunks, chunks]
        out_specs = [in_vmem] + [anywhere] * 3
        kernel = functools.partial(plain_kernel, names)
    results = pl.pallas_call(
        kernel,
        out_shape=[stream, stream] + outs,
        in_specs=[
            pl.BlockSpec(memory_space=pltpu.SMEM), pl.BlockSpec(memory_space=pltpu.SMEM)
        ]
        + [anywhere] * 5,
        out_specs=[anywhere, anywhere] + out_specs,
        scratch_shapes=list(shapes.values()),
        compiler_params=pltpu.CompilerParams(
            vmem_limit_bytes=VMEM_LIMIT, collective_id=0, has_side_effects=True
        ),
        name="layer",
    )(seq_len, live_rows, stream_in, out_grad, norm_gain, first_weight[0], down_weight)
    if reduce:
        share = width // 16
        out, grad, gain_out, first_out, down_out = pl.pallas_call(
                finish_kernel,
                out_shape=[
                    stream,
                    stream,
                    jax.ShapeDtypeStruct((1, share), F32),
                    jax.ShapeDtypeStruct((3 * LANE // 2, width), F32),
                    jax.ShapeDtypeStruct((GROUP, 12 * LANE), F32),
                ],
                in_specs=[anywhere] * 5,
                out_specs=[anywhere, anywhere, in_vmem, anywhere, anywhere],
                scratch_shapes=[
                    pltpu.VMEM((2, rows, width - 1), BF16),
                    pltpu.VMEM((3, width, LANE), F32),
                    pltpu.VMEM((3, 4, GROUP, LANE), F32),
                    pltpu.VMEM((8, width), F32),
                    pltpu.VMEM((3 * LANE // 2, width), F32),
                    pltpu.VMEM((GROUP, 12 * LANE), F32),
                    pltpu.SemaphoreType.DMA((5,)),
                ],
                name="finish",
            )(*results)
        return (out, grad, gain_out, first_out.T[None], down_out.T)
    stream_out, stream_grad, gain, zero, one, two = results

    def columns(chunks, order):
        split = chunks.reshape((3,) + ((2, 4) if order else (4, 2)) + (width, LANE))
        turned = split.transpose((3, 2, 1, 0, 4) if order else (3, 1, 2, 0, 4))
        return turned.reshape(width, 3 * 8 * LANE)

    first_sum = jnp.stack([columns(zero, True), columns(one, True)])
    first_out = lax.psum_scatter(first_sum, "section", scatter_dimension=0, tiled=True)
    first_out = lax.psum_scatter(first_out, "dp", scatter_dimension=2, tiled=True)
    down_sum = columns(two, False).T
    down_out = lax.psum_scatter(down_sum, "section", scatter_dimension=0, tiled=True)
    down_out = lax.psum_scatter(down_out, "dp", scatter_dimension=1, tiled=True)
    gain_out = lax.psum_scatter(gain[:2], "section", scatter_dimension=0, tiled=True)
    gain_out = lax.psum_scatter(gain_out, "dp", scatter_dimension=1, tiled=True)
    return (stream_out, stream_grad, gain_out, first_out.astype(F32), down_out.astype(F32))


def solution(mesh):
    in_specs = (
        P(("dp", "section"), None),
        P("dp"),
        P("dp"),
        P("section", None),
        P("section", None, None),
        P("section", None),
        P(("dp", "section"), None),
    )
    out_specs = (
        P(("dp", "section"), None),
        P(("dp", "section"), None),
        P("section", "dp"),
        P("section", None, "dp"),
        P("section", "dp"),
    )
    return jax.shard_map(
        per_device, mesh=mesh, in_specs=in_specs, out_specs=out_specs, check_vma=False
    )
```
